512 devices in a mesh: row: 32 (over z, y_lo, core), col: 16 (over x, y_hi).
Axes of the slice: x: 4, y: 8 (y_hi: 4, y_lo: 2; y = y_hi * 2 + y_lo), z: 8, core: 2. Of those that a mesh axis runs over, the one named last changes fastest.
Arguments:
- view_a: float32 [128, 512, 768], P('col', 'row'), may hold values from 0.25 to 4
- view_b: float32 [128, 768, 512], P('col', 'row'), may hold values from 0.25 to 4
- estimate: float32 [128, 512, 768], P('col', 'row'), may hold values from 0.5 to 2
- axial_kernel: float32 [2, 31], replicated, may hold values from 0.05 to 1
- lateral_kernel: float32 [2, 2, 11], replicated, may hold values from 0.05 to 1
Outputs:
- restored: float32 [128, 512, 768], P('col', 'row')
The draws below stay inside these ranges and needn't reach their ends.
All inputs are finite; a program needn't handle non-finite values.
Results may differ from the reference program's by a relative error of at most 0.00002.
Values sent between devices are 32-bit elements; how exact they have to be, the bound alone decides.
No kernel may reach another device: no remote copies, remote signals or barrier semaphores. Data moves between devices by JAX's collectives and lax.ppermute only.
A program may use at most 64 MiB of HBM per device.

```python
import math
import jax
import jax.numpy as jnp
from jax import lax

AXIAL = 31
LATERAL = 11
ITERS = 2
NZ = 128
NY = 512
NX = 768


def level_of(rng, shape, shards, smallest, largest):
    loudness, own = 1.0, jax.random.fold_in(rng, 6)
    for position, blocks in shards:
        heights = jnp.exp(jax.random.uniform(jax.random.fold_in(own, position), (blocks,), jnp.float32, smallest / len(shards), largest / len(shards)))
        loudness = loudness * jnp.repeat(heights, shape[position] // blocks).reshape([-1 if axis == position else 1 for axis in range(len(shape))])
    return loudness


def setup_inputs(seed: int = 0) -> dict:
    seeds = jax.random.split(jax.random.key(seed), 6)
    return {
        "view_a": jnp.clip(jnp.exp(math.log(4.0) - 2.7725887 * jax.random.uniform(seeds[0], (NZ, NY, NX), jnp.float32) ** level_of(seeds[0], (NZ, NY, NX), ((0, 16), (1, 32)), -0.2, 0.2)), 0.25, 4.0),
        "view_b": jnp.clip(jnp.exp(math.log(4.0) - 2.7725887 * jax.random.uniform(seeds[1], (NZ, NX, NY), jnp.float32) ** level_of(seeds[1], (NZ, NX, NY), ((0, 16), (1, 32)), -0.2, 0.2)), 0.25, 4.0),
        "estimate": jnp.clip(jnp.exp(math.log(2.0) - 1.3862944 * jax.random.uniform(seeds[2], (NZ, NY, NX), jnp.float32) ** level_of(seeds[2], (NZ, NY, NX), ((0, 16), (1, 32)), -0.2, 0.2)), 0.5, 2.0),
        "axial_kernel": jnp.clip(jnp.exp(jax.random.uniform(seeds[3], (2, AXIAL), jnp.float32, math.log(0.05), math.log(1.0))), 0.05, 1.0),
        "lateral_kernel": jnp.clip(jnp.exp(jax.random.uniform(seeds[4], (2, 2, LATERAL), jnp.float32, math.log(0.05), math.log(1.0))), 0.05, 1.0),
    }


def blur_axis(volume, weights, dimension):
    margin = weights.shape[0] // 2
    extent = volume.shape[dimension]
    padding = [(0, 0), (0, 0), (0, 0)]
    padding[dimension] = (margin, margin)
    padded = jnp.pad(volume, padding)
    summed = weights[0] * lax.slice_in_dim(padded, 0, extent, axis=dimension)
    for offset in range(1, weights.shape[0]):
        summed = summed + weights[offset] * lax.slice_in_dim(padded, offset, offset + extent, axis=dimension)
    return summed


def project(volume, in_plane, axial_weights, depth_weights):
    volume = blur_axis(volume, in_plane, 2)
    volume = blur_axis(volume, axial_weights, 1)
    return blur_axis(volume, depth_weights, 0)


def reference(view_a, view_b, estimate, axial_kernel, lateral_kernel):
    axial = axial_kernel / jnp.sum(axial_kernel, axis=1, keepdims=True)
    lateral = lateral_kernel / jnp.sum(lateral_kernel, axis=2, keepdims=True)
    for iteration in range(ITERS):
        blurred = project(estimate, lateral[0, 1], axial[0], lateral[0, 0])
        quotient = view_a / blurred
        estimate = estimate * project(quotient, lateral[0, 1][::-1], axial[0][::-1], lateral[0, 0][::-1])
        turned = jnp.swapaxes(estimate, 1, 2)
        blurred = project(turned, lateral[1, 1], axial[1], lateral[1, 0])
        quotient = view_b / blurred
        correction = project(quotient, lateral[1, 1][::-1], axial[1][::-1], lateral[1, 0][::-1])
        estimate = estimate * jnp.swapaxes(correction, 1, 2)
    return estimate
```

```python
import functools
import jax
import jax.numpy as jnp
from jax import lax
from jax.experimental import pallas as pl
from jax.experimental.pallas import tpu as pltpu
from jax.sharding import PartitionSpec as P

ITERS = 2
LANES = 128
SHIFT = 64
HIGH = lax.Precision.HIGHEST
VMEM = pl.BlockSpec(memory_space=pltpu.VMEM)
SMEM = pl.BlockSpec(memory_space=pltpu.SMEM)


def splat(value):
    return jnp.full((8, LANES), value, jnp.float32)


def prepare_body(axial_ref, lateral_ref, ya_ref, yb_ref, za_ref, zb_ref, band_ref):
    axial, lateral = axial_ref.shape[1], lateral_ref.shape[2]

    def normalized(read, count):
        taps = [read(k) for k in range(count)]
        total = taps[0]
        for tap in taps[1:]:
            total = total + tap
        total = splat(total)
        return [splat(tap) / total for tap in taps]

    rows = (
        (ya_ref, lambda k: axial_ref[0, k], axial),
        (yb_ref, lambda k: lateral_ref[1, 1, k], lateral),
        (za_ref, lambda k: lateral_ref[0, 0, k], lateral),
        (zb_ref, lambda k: lateral_ref[1, 0, k], lateral),
    )
    for target, read, count in rows:
        for k, tap in enumerate(normalized(read, count)):
            target[k] = tap
    xa = normalized(lambda k: lateral_ref[0, 1, k], lateral)
    xb = normalized(lambda k: axial_ref[1, k], axial)
    lane = lax.broadcasted_iota(jnp.int32, (8, LANES), 1)
    sub = lax.broadcasted_iota(jnp.int32, (8, LANES), 0)

    def fill(step, carry):
        distance = sub + step * 8 - lane - SHIFT
        for index, taps in enumerate((xa, xb)):
            half = len(taps) // 2
            ahead = jnp.zeros((8, LANES), jnp.float32)
            back = jnp.zeros((8, LANES), jnp.float32)
            for k, tap in enumerate(taps):
                ahead = jnp.where(distance == k - half, tap, ahead)
                back = jnp.where(distance == half - k, tap, back)
            at = pl.ds(pl.multiple_of(step * 8, 8), 8)
            band_ref[2 * index, at, :] = ahead
            band_ref[2 * index + 1, at, :] = back
        return carry

    lax.fori_loop(0, 2 * LANES // 8, fill, 0)


def prepare(axial_kernel, lateral_kernel):
    axial, lateral = axial_kernel.shape[1], lateral_kernel.shape[2]
    shapes = [(axial, 8, LANES), (lateral, 8, LANES), (lateral, 8, LANES), (lateral, 8, LANES)]
    shapes.append((4, 2 * LANES, LANES))
    return pl.pallas_call(
        prepare_body,
        out_shape=[jax.ShapeDtypeStruct(shape, jnp.float32) for shape in shapes],
        in_specs=[SMEM, SMEM],
        out_specs=[VMEM] * 5,
        name="prepare",
    )(axial_kernel, lateral_kernel)


def correlate(taps, rows, extent, reverse):
    count = len(taps)
    sums = [None] * extent
    for r in range(extent + count - 1):
        value = rows(r)
        for i in range(max(0, r - count + 1), min(extent, r + 1)):
            k = r - i
            term = taps[count - 1 - k if reverse else k] * value
            sums[i] = term if sums[i] is None else sums[i] + term
    return sums


def padded_rows(low, mid, high, pick):
    margin, extent = low.shape[0], mid.shape[0]

    def rows(r):
        if r < margin:
            return pick(low, r)
        if r < margin + extent:
            return pick(mid, r - margin)
        return pick(high, r - margin - extent)

    return rows


def lanes_at(j):
    return pl.ds(pl.multiple_of(j * LANES, LANES), LANES)


def along_z(taps_ref, low_ref, mid_ref, high_ref, reverse, store):
    rows_y, width = mid_ref.shape[1], mid_ref.shape[2]

    def tile(j, carry):
        lanes = lanes_at(j)
        taps = [taps_ref[k] for k in range(taps_ref.shape[0])]
        for y in range(0, rows_y, 8):
            pick = lambda ref, r: ref[r, y:y + 8, lanes]
            sums = correlate(taps, padded_rows(low_ref, mid_ref, high_ref, pick), mid_ref.shape[0], reverse)
            store(y, j, sums)
        return carry

    lax.fori_loop(0, width // LANES, tile, 0)


def depth_body(reverse, taps_ref, low_ref, mid_ref, high_ref, out_ref):
    def store(y, j, sums):
        out_ref[y:y + 8, :, lanes_at(j)] = jnp.swapaxes(jnp.stack(sums), 0, 1)

    along_z(taps_ref, low_ref, mid_ref, high_ref, reverse, store)


def depth(taps, low, mid, high, reverse):
    nz, ny, nx = mid.shape
    return pl.pallas_call(
        functools.partial(depth_body, reverse),
        out_shape=jax.ShapeDtypeStruct((ny, nz, nx), jnp.float32),
        in_specs=[VMEM] * 4,
        out_specs=VMEM,
        name="depth",
    )(taps, low, mid, high)


def plane_body(reverse, divide, taps_ref, low_ref, mid_ref, high_ref, *refs):
    view_ref, out_ref = refs if divide else (None, refs[0])

    def tile(j, carry):
        lanes = lanes_at(j)
        taps = [taps_ref[k] for k in range(taps_ref.shape[0])]
        pick = lambda ref, r: ref[r, :, lanes]
        sums = correlate(taps, padded_rows(low_ref, mid_ref, high_ref, pick), mid_ref.shape[0], reverse)
        if divide:
            for i, value in enumerate(sums):
                out_ref[i, :, lanes] = view_ref[i, :, lanes] / value
        else:
            for y in range(0, len(sums), 8):
                out_ref[:, y:y + 8, lanes] = jnp.swapaxes(jnp.stack(sums[y:y + 8]), 0, 1)
        return carry

    lax.fori_loop(0, mid_ref.shape[2] // LANES, tile, 0)


def plane(taps, low, mid, high, reverse, view=None):
    ny, nz, nx = mid.shape
    shape = (nz, ny, nx) if view is None else (ny, nz, nx)
    operands = (taps, low, mid, high) + (() if view is None else (view,))
    return pl.pallas_call(
        functools.partial(plane_body, reverse, view is not None),
        out_shape=jax.ShapeDtypeStruct(shape, jnp.float32),
        in_specs=[VMEM] * len(operands),
        out_specs=VMEM,
        name="plane",
    )(*operands)


def clear_edges(wide_ref):
    blank = jnp.zeros((wide_ref.shape[0], LANES), jnp.float32)
    wide_ref[:, :LANES] = blank
    wide_ref[:, wide_ref.shape[1] - LANES:] = blank


def along_x(wide_ref, band):
    width = wide_ref.shape[1] - LANES
    for j in range(width // LANES):
        yield j, jnp.dot(
            wide_ref[:, j * LANES:(j + 2) * LANES], band, precision=HIGH, preferred_element_type=jnp.float32
        )


def first_body(band_ref, estimate_ref, out_ref, wide_ref):
    nz, ny, nx = estimate_ref.shape
    clear_edges(wide_ref)
    wide_ref[:, SHIFT:SHIFT + nx] = estimate_ref[...].reshape(nz * ny, nx)
    for j, value in along_x(wide_ref, band_ref[...]):
        out_ref[:, :, j * LANES:(j + 1) * LANES] = value.reshape(nz, ny, LANES)


def first(band, estimate):
    nz, ny, nx = estimate.shape
    return pl.pallas_call(
        first_body,
        out_shape=jax.ShapeDtypeStruct(estimate.shape, jnp.float32),
        in_specs=[VMEM] * 2,
        out_specs=VMEM,
        scratch_shapes=[pltpu.VMEM((nz * ny, nx + LANES), jnp.float32)],
        name="first",
    )(band, estimate)


def update_body(last, taps_ref, low_ref, mid_ref, high_ref, band_ref, estimate_ref, *refs):
    if last:
        out_ref, wide_ref, mixed_ref = refs
    else:
        next_ref, out_ref, ahead_ref, wide_ref, mixed_ref = refs
    nz, ny, nx = mid_ref.shape

    def store(y, j, sums):
        for z, value in enumerate(sums):
            mixed_ref[z * ny + y:z * ny + y + 8, lanes_at(j)] = value

    along_z(taps_ref, low_ref, mid_ref, high_ref, True, store)
    clear_edges(wide_ref)
    wide_ref[:, SHIFT:SHIFT + nx] = mixed_ref[...]
    for j, value in along_x(wide_ref, band_ref[...]):
        at = slice(j * LANES, (j + 1) * LANES)
        out_ref[:, :, at] = estimate_ref[:, :, at] * value.reshape(nz, ny, LANES)
    if not last:
        wide_ref[:, SHIFT:SHIFT + nx] = out_ref[...].reshape(nz * ny, nx)
        for j, value in along_x(wide_ref, next_ref[...]):
            ahead_ref[:, :, j * LANES:(j + 1) * LANES] = value.reshape(nz, ny, LANES)


def update(taps, low, mid, high, band, estimate, band_next=None):
    nz, ny, nx = mid.shape
    last = band_next is None
    operands = (taps, low, mid, high, band, estimate) + (() if last else (band_next,))
    shape = jax.ShapeDtypeStruct(mid.shape, jnp.float32)
    return pl.pallas_call(
        functools.partial(update_body, last),
        out_shape=[shape] if last else [shape, shape],
        in_specs=[VMEM] * len(operands),
        out_specs=[VMEM] * (1 if last else 2),
        scratch_shapes=[
            pltpu.VMEM((nz * ny, nx + LANES), jnp.float32),
            pltpu.VMEM((nz * ny, nx), jnp.float32),
        ],
        name="update",
    )(*operands)


def exchange(block, axis, width):
    count = lax.axis_size(axis)
    forward = [(i, i + 1) for i in range(count - 1)]
    backward = [(target, source) for source, target in forward]
    extent = block.shape[0]
    low = lax.ppermute(lax.slice_in_dim(block, extent - width, extent, axis=0), axis, forward)
    high = lax.ppermute(lax.slice_in_dim(block, 0, width, axis=0), axis, backward)
    return low, block, high


def reframe(view):
    nz, nx, ny = view.shape
    count = lax.axis_size("row")
    rows = ny // count
    pieces = view.reshape(nz, nx, count, rows).transpose(2, 1, 3, 0).reshape(count, nx, rows * nz)
    arrived = lax.all_to_all(pieces, "row", 0, 0, tiled=True)
    return arrived.reshape(count * nx, rows * nz).T.reshape(rows, nz, count * nx)


def per_device(view_a, view_b, estimate, axial_kernel, lateral_kernel):
    ya, yb, za, zb, bands = prepare(axial_kernel, lateral_kernel)
    views = (jnp.swapaxes(view_a, 0, 1), reframe(view_b))
    ytaps, ztaps = (ya, yb), (za, zb)
    ahead = first(bands[0], estimate)
    steps = 2 * ITERS
    for step in range(steps):
        v = step % 2
        yt, zt, view = ytaps[v], ztaps[v], views[v]
        margin = yt.shape[0] // 2
        blurred = depth(zt, *exchange(ahead, "col", zt.shape[0] // 2), False)
        quotient = plane(yt, *exchange(blurred, "row", margin), False, view)
        spread = plane(yt, *exchange(quotient, "row", margin), True)
        halo = exchange(spread, "col", zt.shape[0] // 2)
        if step == steps - 1:
            (estimate,) = update(zt, *halo, bands[2 * v + 1], estimate)
        else:
            estimate, ahead = update(zt, *halo, bands[2 * v + 1], estimate, bands[2 * (1 - v)])
    return estimate


def solution(mesh):
    in_specs = (P("col", "row", None), P("col", "row", None), P("col", "row", None), P(), P())
    out_specs = P("col", "row", None)
    return jax.shard_map(
        per_device, mesh=mesh, in_specs=in_specs, out_specs=out_specs, check_vma=False
    )
```

```python
import functools
import jax
import jax.numpy as jnp
from jax import lax
from jax.experimental import pallas as pl
from jax.experimental.pallas import tpu as pltpu
from jax.sharding import PartitionSpec as P

ITERS = 2
LANES = 128
SHIFT = 64
CHUNKS = 1
CHUNK_LIMIT = 8 * 2**20
HIGH = lax.Precision.HIGHEST
VMEM = pl.BlockSpec(memory_space=pltpu.VMEM)
LIMIT = pltpu.CompilerParams(vmem_limit_bytes=CHUNK_LIMIT)
SMEM = pl.BlockSpec(memory_space=pltpu.SMEM)


def splat(value):
    return jnp.full((8, LANES), value, jnp.float32)


def prepare_body(axial_ref, lateral_ref, ya_ref, yb_ref, za_ref, zb_ref, *band_refs):
    axial, lateral = axial_ref.shape[1], lateral_ref.shape[2]

    def normalized(read, count):
        taps = [read(k) for k in range(count)]
        total = taps[0]
        for tap in taps[1:]:
            total = total + tap
        total = splat(total)
        return [splat(tap) / total for tap in taps]

    rows = (
        (ya_ref, lambda k: axial_ref[0, k], axial),
        (yb_ref, lambda k: lateral_ref[1, 1, k], lateral),
        (za_ref, lambda k: lateral_ref[0, 0, k], lateral),
        (zb_ref, lambda k: lateral_ref[1, 0, k], lateral),
    )
    for target, read, count in rows:
        for k, tap in enumerate(normalized(read, count)):
            target[k] = tap
    xa = normalized(lambda k: lateral_ref[0, 1, k], lateral)
    xb = normalized(lambda k: axial_ref[1, k], axial)
    lane = lax.broadcasted_iota(jnp.int32, (8, LANES), 1)
    sub = lax.broadcasted_iota(jnp.int32, (8, LANES), 0)

    def fill(step, carry):
        distance = sub + step * 8 - lane - SHIFT
        for index, taps in enumerate((xa, xb)):
            half = len(taps) // 2
            ahead = jnp.zeros((8, LANES), jnp.float32)
            back = jnp.zeros((8, LANES), jnp.float32)
            for k, tap in enumerate(taps):
                ahead = jnp.where(distance == k - half, tap, ahead)
                back = jnp.where(distance == half - k, tap, back)
            at = pl.ds(pl.multiple_of(step * 8, 8), 8)
            band_refs[2 * index][at, :] = ahead
            band_refs[2 * index + 1][at, :] = back
        return carry

    lax.fori_loop(0, 2 * LANES // 8, fill, 0)


def local(*shape):
    return pltpu.VMEM(shape, jnp.float32)


def call(body, name, operands, shapes, scratch=()):
    operands = [pltpu.with_memory_space_constraint(operand, pltpu.VMEM) for operand in operands]
    return pl.pallas_call(
        body,
        out_shape=shapes,
        in_specs=[VMEM] * len(operands),
        out_specs=[VMEM] * len(shapes),
        scratch_shapes=scratch,
        compiler_params=LIMIT,
        name=name,
    )(*operands)


def prepare(axial_kernel, lateral_kernel):
    axial, lateral = axial_kernel.shape[1], lateral_kernel.shape[2]
    shapes = [local(count, 8, LANES) for count in (axial, lateral, lateral, lateral)]
    shapes += [local(2 * LANES, LANES)] * 4
    outs = pl.pallas_call(
        prepare_body,
        out_shape=shapes,
        in_specs=[SMEM, SMEM],
        out_specs=[VMEM] * len(shapes),
        compiler_params=LIMIT,
        name="prepare",
    )(axial_kernel, lateral_kernel)
    return outs[:2], outs[2:4], (outs[4:6], outs[6:8])


def correlate(taps, rows, extent, reverse):
    count = len(taps)
    sums = [None] * extent
    for r in range(extent + count - 1):
        value = rows(r)
        for i in range(max(0, r - count + 1), min(extent, r + 1)):
            k = r - i
            term = taps[count - 1 - k if reverse else k] * value
            sums[i] = term if sums[i] is None else sums[i] + term
    return sums


def padded_rows(low, mid, high, pick):
    margin, extent = low.shape[0], mid.shape[0]

    def rows(r):
        if r < margin:
            return pick(low, r)
        if r < margin + extent:
            return pick(mid, r - margin)
        return pick(high, r - margin - extent)

    return rows


def lanes_at(j):
    return pl.ds(pl.multiple_of(j * LANES, LANES), LANES)


def put(out_refs, i, at, lanes, value):
    mid_ref, first_ref, last_ref = out_refs
    extent, margin = mid_ref.shape[0], first_ref.shape[0]
    mid_ref[i, at, lanes] = value
    if i < margin:
        first_ref[i, at, lanes] = value
    if i >= extent - margin:
        last_ref[i - extent + margin, at, lanes] = value


def along_z(taps_ref, low_ref, mid_ref, high_ref, reverse, store):
    rows_y, width = mid_ref.shape[1], mid_ref.shape[2]

    def tile(j, carry):
        lanes = lanes_at(j)
        taps = [taps_ref[k] for k in range(taps_ref.shape[0])]
        for y in range(0, rows_y, 8):
            pick = lambda ref, r: ref[r, y:y + 8, lanes]
            sums = correlate(taps, padded_rows(low_ref, mid_ref, high_ref, pick), mid_ref.shape[0], reverse)
            store(y, j, sums)
        return carry

    lax.fori_loop(0, width // LANES, tile, 0)


def depth_body(reverse, taps_ref, low_ref, mid_ref, high_ref, *out_refs):
    def store(y, j, sums):
        turned = jnp.swapaxes(jnp.stack(sums), 0, 1)
        for i in range(8):
            put(out_refs, y + i, slice(None), lanes_at(j), turned[i])

    along_z(taps_ref, low_ref, mid_ref, high_ref, reverse, store)


def depth(taps, low, mid, high, reverse, margin):
    nz, ny, nx = mid.shape
    shapes = [local(ny, nz, nx), local(margin, nz, nx), local(margin, nz, nx)]
    return call(functools.partial(depth_body, reverse), "depth", (taps, low, mid, high), shapes)


def plane_body(reverse, divide, taps_ref, low_ref, mid_ref, high_ref, *refs):
    view_ref, out_refs = (refs[0], refs[1:]) if divide else (None, refs)

    def tile(j, carry):
        lanes = lanes_at(j)
        taps = [taps_ref[k] for k in range(taps_ref.shape[0])]
        pick = lambda ref, r: ref[r, :, lanes]
        sums = correlate(taps, padded_rows(low_ref, mid_ref, high_ref, pick), mid_ref.shape[0], reverse)
        if divide:
            for i, value in enumerate(sums):
                put(out_refs, i, slice(None), lanes, view_ref[i, :, lanes] / value)
        else:
            for y in range(0, len(sums), 8):
                turned = jnp.swapaxes(jnp.stack(sums[y:y + 8]), 0, 1)
                for z in range(8):
                    put(out_refs, z, slice(y, y + 8), lanes, turned[z])
        return carry

    lax.fori_loop(0, mid_ref.shape[2] // LANES, tile, 0)


def plane(taps, low, mid, high, reverse, margin, view=None):
    ny, nz, nx = mid.shape
    outer, inner = (nz, ny) if view is None else (ny, nz)
    shapes = [local(outer, inner, nx), local(margin, inner, nx), local(margin, inner, nx)]
    operands = (taps, low, mid, high) + (() if view is None else (view,))
    return call(functools.partial(plane_body, reverse, view is not None), "plane", operands, shapes)


def clear_edges(wide_ref):
    blank = jnp.zeros((wide_ref.shape[0], LANES), jnp.float32)
    wide_ref[:, :LANES] = blank
    wide_ref[:, wide_ref.shape[1] - LANES:] = blank


def along_x(wide_ref, band):
    width = wide_ref.shape[1] - LANES
    for j in range(width // LANES):
        yield j, jnp.dot(
            wide_ref[:, j * LANES:(j + 2) * LANES], band, precision=HIGH, preferred_element_type=jnp.float32
        )


def put_ahead(wide_ref, band_ref, out_refs, ny):
    per_chunk = out_refs[0].shape[2] // LANES
    for j, value in along_x(wide_ref, band_ref[...]):
        chunk, inside = divmod(j, per_chunk)
        refs = out_refs[3 * chunk:3 * chunk + 3]
        lanes = slice(inside * LANES, (inside + 1) * LANES)
        for z in range(refs[0].shape[0]):
            put(refs, z, slice(None), lanes, value[z * ny:(z + 1) * ny])


def first_body(band_ref, estimate_ref, *refs):
    out_refs, wide_ref = refs[:-1], refs[-1]
    nz, ny, nx = estimate_ref.shape
    clear_edges(wide_ref)
    wide_ref[:, SHIFT:SHIFT + nx] = estimate_ref[...].reshape(nz * ny, nx)
    put_ahead(wide_ref, band_ref, out_refs, ny)


def ahead_shapes(shape, margin):
    nz, ny, nx = shape
    part = nx // CHUNKS
    return [local(nz, ny, part), local(margin, ny, part), local(margin, ny, part)] * CHUNKS


def chunked(outs):
    return [tuple(outs[3 * c:3 * c + 3]) for c in range(CHUNKS)]


def first(band, estimate, margin):
    nz, ny, nx = estimate.shape
    shapes = ahead_shapes(estimate.shape, margin)
    scratch = [local(nz * ny, nx + LANES)]
    return chunked(call(first_body, "first", (band, estimate), shapes, scratch))


def update_body(last, taps_ref, band_ref, estimate_ref, *refs):
    halo_refs, refs = refs[:3 * CHUNKS], refs[3 * CHUNKS:]
    refs, (wide_ref, mixed_ref) = refs[:-2], refs[-2:]
    if last:
        (out_ref,) = refs
    else:
        next_ref, out_ref, *ahead_refs = refs
    nz, ny, nx = estimate_ref.shape
    per_chunk = nx // CHUNKS // LANES
    for c in range(CHUNKS):
        def store(y, j, sums):
            for z, value in enumerate(sums):
                mixed_ref[z * ny + y:z * ny + y + 8, lanes_at(j + c * per_chunk)] = value

        along_z(taps_ref, *halo_refs[3 * c:3 * c + 3], True, store)
    clear_edges(wide_ref)
    wide_ref[:, SHIFT:SHIFT + nx] = mixed_ref[...]
    for j, value in along_x(wide_ref, band_ref[...]):
        at = slice(j * LANES, (j + 1) * LANES)
        out_ref[:, :, at] = estimate_ref[:, :, at] * value.reshape(nz, ny, LANES)
    if not last:
        wide_ref[:, SHIFT:SHIFT + nx] = out_ref[...].reshape(nz * ny, nx)
        put_ahead(wide_ref, next_ref, ahead_refs, ny)


def update(taps, halos, band, estimate, band_next=None):
    nz, ny, nx = estimate.shape
    last = band_next is None
    operands = (taps, band, estimate) + sum(halos, ()) + (() if last else (band_next,))
    shapes = [local(nz, ny, nx)]
    if last:
        shapes = [jax.ShapeDtypeStruct((nz, ny, nx), jnp.float32)]
    else:
        shapes += ahead_shapes(estimate.shape, taps.shape[0] // 2)
    scratch = [local(nz * ny, nx + LANES), local(nz * ny, nx)]
    outs = call(functools.partial(update_body, last), "update", operands, shapes, scratch)
    return outs[0], (None if last else chunked(outs[1:]))


def exchange(parts, axis):
    block, first_rows, last_rows = parts
    count = lax.axis_size(axis)
    forward = [(i, i + 1) for i in range(count - 1)]
    backward = [(target, source) for source, target in forward]
    low = lax.ppermute(last_rows, axis, forward)
    high = lax.ppermute(first_rows, axis, backward)
    return low, block, high


def reframe(view):
    nz, nx, ny = view.shape
    count = lax.axis_size("row")
    rows = ny // count
    pieces = view.reshape(nz, nx, count, rows).transpose(2, 1, 3, 0).reshape(count, nx, rows * nz)
    arrived = lax.all_to_all(pieces, "row", 0, 0, tiled=True)
    return arrived.reshape(count * nx, rows * nz).T.reshape(rows, nz, count * nx)


def per_device(view_a, view_b, estimate, axial_kernel, lateral_kernel):
    ytaps, ztaps, bands = prepare(axial_kernel, lateral_kernel)
    views = (jnp.swapaxes(view_a, 0, 1), reframe(view_b))
    views = [jnp.split(view, CHUNKS, axis=2) for view in views]
    depth_margin = lateral_kernel.shape[2] // 2
    ahead = first(bands[0][0], estimate, depth_margin)
    steps = 2 * ITERS
    for step in range(steps):
        v = step % 2
        yt, zt = ytaps[v], ztaps[v]
        margin = yt.shape[0] // 2
        ahead = [depth(zt, *exchange(parts, "col"), False, margin) for parts in ahead]
        ahead = [
            plane(yt, *exchange(parts, "row"), False, margin, view) for parts, view in zip(ahead, views[v])
        ]
        ahead = [plane(yt, *exchange(parts, "row"), True, depth_margin) for parts in ahead]
        halos = [exchange(parts, "col") for parts in ahead]
        band_next = None if step == steps - 1 else bands[1 - v][0]
        estimate, ahead = update(zt, halos, bands[v][1], estimate, band_next)
    return estimate


def solution(mesh):
    in_specs = (P("col", "row", None), P("col", "row", None), P("col", "row", None), P(), P())
    out_specs = P("col", "row", None)
    return jax.shard_map(
        per_device, mesh=mesh, in_specs=in_specs, out_specs=out_specs, check_vma=False
    )
```

```python
import functools
import jax
import jax.numpy as jnp
from jax import lax
from jax.experimental import pallas as pl
from jax.experimental.pallas import tpu as pltpu
from jax.sharding import PartitionSpec as P

ITERS = 2
LANES = 128
SHIFT = 64
CHUNKS = 1
CHUNK_LIMIT = 8 * 2**20
HIGH = lax.Precision.HIGHEST
VMEM = pl.BlockSpec(memory_space=pltpu.VMEM)
LIMIT = pltpu.CompilerParams(vmem_limit_bytes=CHUNK_LIMIT)
SMEM = pl.BlockSpec(memory_space=pltpu.SMEM)


def splat(value):
    return jnp.full((8, LANES), value, jnp.float32)


def normalized(read, count):
    taps = [read(k) for k in range(count)]
    total = taps[0]
    for tap in taps[1:]:
        total = total + tap
    total = splat(total)
    return [splat(tap) / total for tap in taps]


def fill_band(band_ref, taps, sign):
    half = len(taps) // 2
    lane = lax.broadcasted_iota(jnp.int32, (8, LANES), 1)
    sub = lax.broadcasted_iota(jnp.int32, (8, LANES), 0)

    def fill(step, carry):
        distance = sign * (sub + step * 8 - lane - SHIFT)
        value = jnp.zeros((8, LANES), jnp.float32)
        for k, tap in enumerate(taps):
            value = jnp.where(distance == k - half, tap, value)
        band_ref[pl.ds(pl.multiple_of(step * 8, 8), 8), :] = value
        return carry

    lax.fori_loop(0, 2 * LANES // 8, fill, 0, unroll=8)


def prepare_body(axial_ref, lateral_ref, ya_ref, yb_ref, za_ref, zb_ref, *band_refs):
    axial, lateral = axial_ref.shape[1], lateral_ref.shape[2]
    rows = (
        (ya_ref, lambda k: axial_ref[0, k], axial),
        (yb_ref, lambda k: lateral_ref[1, 1, k], lateral),
        (za_ref, lambda k: lateral_ref[0, 0, k], lateral),
        (zb_ref, lambda k: lateral_ref[1, 0, k], lateral),
    )
    for target, read, count in rows:
        for k, tap in enumerate(normalized(read, count)):
            target[k] = tap
    xa = normalized(lambda k: lateral_ref[0, 1, k], lateral)
    xb = normalized(lambda k: axial_ref[1, k], axial)
    for taps, refs in ((xa, band_refs[:2]), (xb, band_refs[2:])):
        fill_band(refs[0], taps, 1)
        fill_band(refs[1], taps, -1)


def local(*shape):
    return pltpu.VMEM(shape, jnp.float32)


def call(body, operands, shapes, scratch=()):
    operands = [pltpu.with_memory_space_constraint(operand, pltpu.VMEM) for operand in operands]
    return pl.pallas_call(
        body,
        out_shape=shapes,
        in_specs=[VMEM] * len(operands),
        out_specs=[VMEM] * len(shapes),
        scratch_shapes=scratch,
        compiler_params=LIMIT,
    )(*operands)


def prepare(axial_kernel, lateral_kernel):
    axial, lateral = axial_kernel.shape[1], lateral_kernel.shape[2]
    shapes = [local(count, 8, LANES) for count in (axial, lateral, lateral, lateral)]
    shapes += [local(2 * LANES, LANES)] * 4
    outs = pl.pallas_call(
        prepare_body,
        out_shape=shapes,
        in_specs=[SMEM, SMEM],
        out_specs=[VMEM] * len(shapes),
        compiler_params=LIMIT,
        name="prepare",
    )(axial_kernel, lateral_kernel)
    return outs[:2], outs[2:4], (outs[4:6], outs[6:8])


def correlate(taps, rows, extent, reverse):
    count = len(taps)
    sums = [None] * extent
    for r in range(extent + count - 1):
        value = rows(r)
        for i in range(max(0, r - count + 1), min(extent, r + 1)):
            k = r - i
            term = taps[count - 1 - k if reverse else k] * value
            sums[i] = term if sums[i] is None else sums[i] + term
    return sums


def padded_rows(low, mid, high, pick):
    margin, extent = low.shape[0], mid.shape[0]

    def rows(r):
        if r < margin:
            return pick(low, r)
        if r < margin + extent:
            return pick(mid, r - margin)
        return pick(high, r - margin - extent)

    return rows


def lanes_at(j):
    return pl.ds(pl.multiple_of(j * LANES, LANES), LANES)


def put(out_refs, i, at, lanes, value):
    mid_ref, first_ref, last_ref = out_refs
    extent, margin = mid_ref.shape[0], first_ref.shape[0]
    mid_ref[i, at, lanes] = value
    if i < margin:
        first_ref[i, at, lanes] = value
    if i >= extent - margin:
        last_ref[i - extent + margin, at, lanes] = value


def along_z(taps_ref, low_ref, mid_ref, high_ref, reverse, store):
    rows_y, width = mid_ref.shape[1], mid_ref.shape[2]

    def tile(j, carry):
        lanes = lanes_at(j)
        taps = [taps_ref[k] for k in range(taps_ref.shape[0])]
        for y in range(0, rows_y, 8):
            pick = lambda ref, r: ref[r, y:y + 8, lanes]
            sums = correlate(taps, padded_rows(low_ref, mid_ref, high_ref, pick), mid_ref.shape[0], reverse)
            store(y, j, sums)
        return carry

    lax.fori_loop(0, width // LANES, tile, 0)


def depth_body(reverse, taps_ref, low_ref, mid_ref, high_ref, *out_refs):
    def store(y, j, sums):
        turned = jnp.swapaxes(jnp.stack(sums), 0, 1)
        for i in range(8):
            put(out_refs, y + i, slice(None), lanes_at(j), turned[i])

    along_z(taps_ref, low_ref, mid_ref, high_ref, reverse, store)


def depth(taps, low, mid, high, reverse, margin):
    nz, ny, nx = mid.shape
    shapes = [local(ny, nz, nx), local(margin, nz, nx), local(margin, nz, nx)]
    return call(functools.partial(depth_body, reverse), (taps, low, mid, high), shapes)


def plane_body(reverse, divide, taps_ref, low_ref, mid_ref, high_ref, *refs):
    view_ref, out_refs = (refs[0], refs[1:]) if divide else (None, refs)

    def tile(j, carry):
        lanes = lanes_at(j)
        taps = [taps_ref[k] for k in range(taps_ref.shape[0])]
        pick = lambda ref, r: ref[r, :, lanes]
        sums = correlate(taps, padded_rows(low_ref, mid_ref, high_ref, pick), mid_ref.shape[0], reverse)
        if divide:
            for i, value in enumerate(sums):
                put(out_refs, i, slice(None), lanes, view_ref[i, :, lanes] / value)
        else:
            for y in range(0, len(sums), 8):
                turned = jnp.swapaxes(jnp.stack(sums[y:y + 8]), 0, 1)
                for z in range(8):
                    put(out_refs, z, slice(y, y + 8), lanes, turned[z])
        return carry

    lax.fori_loop(0, mid_ref.shape[2] // LANES, tile, 0)


def plane(taps, low, mid, high, reverse, margin, view=None):
    ny, nz, nx = mid.shape
    outer, inner = (nz, ny) if view is None else (ny, nz)
    shapes = [local(outer, inner, nx), local(margin, inner, nx), local(margin, inner, nx)]
    operands = (taps, low, mid, high) + (() if view is None else (view,))
    return call(functools.partial(plane_body, reverse, view is not None), operands, shapes)


def deep_body(taps_ref, low_ref, mid_ref, high_ref, view_low_ref, view_ref, view_high_ref, *out_refs):
    extent = mid_ref.shape[0]

    def tile(j, carry):
        lanes = lanes_at(j)
        taps = [taps_ref[k] for k in range(taps_ref.shape[0])]
        pick = lambda ref, r: ref[r, :, lanes]
        wide = extent + len(taps) - 1
        sums = correlate(taps, padded_rows(low_ref, mid_ref, high_ref, pick), wide, False)
        seen = padded_rows(view_low_ref, view_ref, view_high_ref, pick)
        quotient = [seen(r) / value for r, value in enumerate(sums)]
        sums = correlate(taps, lambda r: quotient[r], extent, True)
        for y in range(0, extent, 8):
            turned = jnp.swapaxes(jnp.stack(sums[y:y + 8]), 0, 1)
            for z in range(8):
                put(out_refs, z, slice(y, y + 8), lanes, turned[z])
        return carry

    lax.fori_loop(0, mid_ref.shape[2] // LANES, tile, 0)


def deep(taps, halo, view, margin):
    ny, nz, nx = halo[1].shape
    shapes = [local(nz, ny, nx), local(margin, ny, nx), local(margin, ny, nx)]
    return call(deep_body, (taps, *halo, *view), shapes)


def clear_edges(wide_ref):
    blank = jnp.zeros((wide_ref.shape[0], LANES), jnp.float32)
    wide_ref[:, :LANES] = blank
    wide_ref[:, wide_ref.shape[1] - LANES:] = blank


def along_x(wide_ref, band):
    width = wide_ref.shape[1] - LANES
    for j in range(width // LANES):
        yield j, jnp.dot(
            wide_ref[:, j * LANES:(j + 2) * LANES], band, precision=HIGH, preferred_element_type=jnp.float32
        )


def put_ahead(wide_ref, band_ref, out_refs, ny):
    per_chunk = out_refs[0].shape[2] // LANES
    for j, value in along_x(wide_ref, band_ref[...]):
        chunk, inside = divmod(j, per_chunk)
        refs = out_refs[3 * chunk:3 * chunk + 3]
        lanes = slice(inside * LANES, (inside + 1) * LANES)
        for z in range(refs[0].shape[0]):
            put(refs, z, slice(None), lanes, value[z * ny:(z + 1) * ny])


def first_body(lateral_ref, estimate_ref, *refs):
    out_refs, (wide_ref, band_ref) = refs[:-2], refs[-2:]
    nz, ny, nx = estimate_ref.shape
    count = lateral_ref.shape[2]
    fill_band(band_ref, normalized(lambda k: lateral_ref[0, 1, k], count), 1)
    clear_edges(wide_ref)
    wide_ref[:, SHIFT:SHIFT + nx] = estimate_ref[...].reshape(nz * ny, nx)
    put_ahead(wide_ref, band_ref, out_refs, ny)


def ahead_shapes(shape, margin):
    nz, ny, nx = shape
    part = nx // CHUNKS
    return [local(nz, ny, part), local(margin, ny, part), local(margin, ny, part)] * CHUNKS


def chunked(outs):
    return [tuple(outs[3 * c:3 * c + 3]) for c in range(CHUNKS)]


def first(lateral_kernel, estimate, margin):
    nz, ny, nx = estimate.shape
    shapes = ahead_shapes(estimate.shape, margin)
    outs = pl.pallas_call(
        first_body,
        out_shape=shapes,
        in_specs=[SMEM, VMEM],
        out_specs=[VMEM] * len(shapes),
        scratch_shapes=[local(nz * ny, nx + LANES), local(2 * LANES, LANES)],
        compiler_params=LIMIT,
        name="first",
    )(lateral_kernel, pltpu.with_memory_space_constraint(estimate, pltpu.VMEM))
    return chunked(outs)


def update_body(last, taps_ref, band_ref, estimate_ref, *refs):
    halo_refs, refs = refs[:3 * CHUNKS], refs[3 * CHUNKS:]
    refs, (wide_ref, mixed_ref) = refs[:-2], refs[-2:]
    if last:
        (out_ref,) = refs
    else:
        next_ref, out_ref, *ahead_refs = refs
    nz, ny, nx = estimate_ref.shape
    per_chunk = nx // CHUNKS // LANES
    for c in range(CHUNKS):
        def store(y, j, sums):
            for z, value in enumerate(sums):
                mixed_ref[z * ny + y:z * ny + y + 8, lanes_at(j + c * per_chunk)] = value

        along_z(taps_ref, *halo_refs[3 * c:3 * c + 3], True, store)
    clear_edges(wide_ref)
    wide_ref[:, SHIFT:SHIFT + nx] = mixed_ref[...]
    for j, value in along_x(wide_ref, band_ref[...]):
        at = slice(j * LANES, (j + 1) * LANES)
        out_ref[:, :, at] = estimate_ref[:, :, at] * value.reshape(nz, ny, LANES)
    if not last:
        wide_ref[:, SHIFT:SHIFT + nx] = out_ref[...].reshape(nz * ny, nx)
        put_ahead(wide_ref, next_ref, ahead_refs, ny)


def update(taps, halos, band, estimate, band_next=None):
    nz, ny, nx = estimate.shape
    last = band_next is None
    operands = (taps, band, estimate) + sum(halos, ()) + (() if last else (band_next,))
    shapes = [local(nz, ny, nx)]
    if last:
        shapes = [jax.ShapeDtypeStruct((nz, ny, nx), jnp.float32)]
    else:
        shapes += ahead_shapes(estimate.shape, taps.shape[0] // 2)
    scratch = [local(nz * ny, nx + LANES), local(nz * ny, nx)]
    outs = call(functools.partial(update_body, last), operands, shapes, scratch)
    return outs[0], (None if last else chunked(outs[1:]))


def exchange(parts, axis):
    block, first_rows, last_rows = parts
    count = lax.axis_size(axis)
    forward = [(i, i + 1) for i in range(count - 1)]
    backward = [(target, source) for source, target in forward]
    low = lax.ppermute(last_rows, axis, forward)
    high = lax.ppermute(first_rows, axis, backward)
    return low, block, high


def pack_body(view_ref, out_ref):
    nz, nx, ny = view_ref.shape
    group = LANES // nz
    slot = lax.broadcasted_iota(jnp.int32, (8, LANES), 1) // group

    def tile(step, carry):
        t, at = step // (nx // 8), pl.ds(pl.multiple_of(step % (nx // 8) * 8, 8), 8)
        parts = [view_ref[z, at, lanes_at(t)] for z in range(nz)]
        span = nz // 2
        while span:
            odd = (slot & span) != 0
            for z in range(nz):
                if not z & span:
                    one, two = parts[z], parts[z + span]
                    parts[z] = jnp.where(odd, pltpu.roll(two, group * span, 1), one)
                    parts[z + span] = jnp.where(odd, two, pltpu.roll(one, LANES - group * span, 1))
            span //= 2
        for z in range(nz):
            out_ref[t * nz + z, at, :] = parts[z]
        return carry

    lax.fori_loop(0, ny // LANES * (nx // 8), tile, 0, unroll=True)


def unpack_body(arrived_ref, *out_refs):
    count, nx = arrived_ref.shape[0], arrived_ref.shape[1]
    nz, ny = out_refs[0].shape[1], out_refs[0].shape[0]
    flat = arrived_ref[...].reshape(count * nx, LANES)
    for j in range(count * nx // LANES):
        lanes = slice(j * LANES, (j + 1) * LANES)
        turned = jnp.swapaxes(flat[lanes].T.reshape(nz, ny, LANES), 0, 1)
        for y in range(ny):
            put(out_refs, y, slice(None), lanes, turned[y])


def reframe(view, margin):
    nz, nx, ny = view.shape
    count = lax.axis_size("row")
    rows = ny // count
    (pieces,) = call(pack_body, (view,), [local(count, nx, rows * nz)])
    arrived = lax.all_to_all(pieces, "row", 0, 0, tiled=True)
    shapes = [local(rows, nz, count * nx), local(margin, nz, count * nx), local(margin, nz, count * nx)]
    return call(unpack_body, (arrived,), shapes)


def per_device(view_a, view_b, estimate, axial_kernel, lateral_kernel):
    margin_a, margin = axial_kernel.shape[1] // 2, lateral_kernel.shape[2] // 2
    seen_a = jnp.swapaxes(view_a, 0, 1)
    seen_b = exchange(reframe(view_b, margin), "row")
    ytaps, ztaps, bands = prepare(axial_kernel, lateral_kernel)
    (ahead,) = first(lateral_kernel, estimate, margin)
    steps = 2 * ITERS
    for step in range(steps):
        v = step % 2
        yt, zt = ytaps[v], ztaps[v]
        ahead = depth(zt, *exchange(ahead, "col"), False, 2 * margin if v else margin_a)
        if v:
            ahead = deep(yt, exchange(ahead, "row"), seen_b, margin)
        else:
            ahead = plane(yt, *exchange(ahead, "row"), False, margin_a, seen_a)
            ahead = plane(yt, *exchange(ahead, "row"), True, margin)
        halo = exchange(ahead, "col")
        if step == steps - 1:
            estimate, _ = update(zt, [halo], bands[v][1], estimate)
        else:
            estimate, (ahead,) = update(zt, [halo], bands[v][1], estimate, bands[1 - v][0])
    return estimate


def solution(mesh):
    in_specs = (P("col", "row", None), P("col", "row", None), P("col", "row", None), P(), P())
    out_specs = P("col", "row", None)
    return jax.shard_map(
        per_device, mesh=mesh, in_specs=in_specs, out_specs=out_specs, check_vma=False
    )
```

```python
import functools
import jax
import jax.numpy as jnp
from jax import lax
from jax.experimental import pallas as pl
from jax.experimental.pallas import tpu as pltpu
from jax.sharding import PartitionSpec as P

ITERS = 2
LANES = 128
SHIFT = 64
CHUNKS = 1
CHUNK_LIMIT = 8 * 2**20
VMEM = pl.BlockSpec(memory_space=pltpu.VMEM)
LIMIT = pltpu.CompilerParams(vmem_limit_bytes=CHUNK_LIMIT)
SMEM = pl.BlockSpec(memory_space=pltpu.SMEM)


def splat(value):
    return jnp.full((8, LANES), value, jnp.float32)


def normalized(read, count):
    taps = [read(k) for k in range(count)]
    total = taps[0]
    for tap in taps[1:]:
        total = total + tap
    total = splat(total)
    return [splat(tap) / total for tap in taps]


def fill_band(band_ref, taps, sign):
    half = len(taps) // 2
    lane = lax.broadcasted_iota(jnp.int32, (8, LANES), 1)
    sub = lax.broadcasted_iota(jnp.int32, (8, LANES), 0)

    def fill(step, carry):
        distance = sign * (sub + step * 8 - lane - SHIFT)
        value = jnp.zeros((8, LANES), jnp.float32)
        for k, tap in enumerate(taps):
            value = jnp.where(distance == k - half, tap, value)
        band_ref[pl.ds(pl.multiple_of(step * 8, 8), 8), :] = value
        return carry

    lax.fori_loop(0, 2 * LANES // 8, fill, 0, unroll=8)


def halves(value):
    high = value.astype(jnp.bfloat16)
    return high, (value - high.astype(jnp.float32)).astype(jnp.bfloat16)


def split_band(wide_ref, out_ref):
    out_ref[:, :LANES], out_ref[:, LANES:] = halves(wide_ref[...])


def prepare_body(axial_ref, lateral_ref, ya_ref, yb_ref, za_ref, zb_ref, *band_refs):
    band_refs, full_ref = band_refs[:-1], band_refs[-1]
    axial, lateral = axial_ref.shape[1], lateral_ref.shape[2]
    rows = (
        (ya_ref, lambda k: axial_ref[0, k], axial),
        (yb_ref, lambda k: lateral_ref[1, 1, k], lateral),
        (za_ref, lambda k: lateral_ref[0, 0, k], lateral),
        (zb_ref, lambda k: lateral_ref[1, 0, k], lateral),
    )
    for target, read, count in rows:
        for k, tap in enumerate(normalized(read, count)):
            target[k] = tap
    xa = normalized(lambda k: lateral_ref[0, 1, k], lateral)
    xb = normalized(lambda k: axial_ref[1, k], axial)
    for taps, refs in ((xa, band_refs[:2]), (xb, band_refs[2:])):
        for ref, sign in zip(refs, (1, -1)):
            fill_band(full_ref, taps, sign)
            split_band(full_ref, ref)


def local(*shape):
    return pltpu.VMEM(shape, jnp.float32)


def call(body, operands, shapes, scratch=()):
    operands = [pltpu.with_memory_space_constraint(operand, pltpu.VMEM) for operand in operands]
    return pl.pallas_call(
        body,
        out_shape=shapes,
        in_specs=[VMEM] * len(operands),
        out_specs=[VMEM] * len(shapes),
        scratch_shapes=scratch,
        compiler_params=LIMIT,
    )(*operands)


def prepare(axial_kernel, lateral_kernel):
    axial, lateral = axial_kernel.shape[1], lateral_kernel.shape[2]
    shapes = [local(count, 8, LANES) for count in (axial, lateral, lateral, lateral)]
    shapes += [pltpu.VMEM((2 * LANES, 2 * LANES), jnp.bfloat16)] * 4
    outs = pl.pallas_call(
        prepare_body,
        out_shape=shapes,
        in_specs=[SMEM, SMEM],
        out_specs=[VMEM] * len(shapes),
        scratch_shapes=[local(2 * LANES, LANES)],
        compiler_params=LIMIT,
        name="prepare",
    )(axial_kernel, lateral_kernel)
    return outs[:2], outs[2:4], (outs[4:6], outs[6:8])


def correlate(taps, rows, extent, reverse, begun=None):
    count = len(taps)
    sums = [None] * extent
    for r in range(extent + count - 1):
        value = rows(r)
        if value is None:
            continue
        for i in range(max(0, r - count + 1), min(extent, r + 1)):
            k = r - i
            term = taps[count - 1 - k if reverse else k] * value
            if sums[i] is None and begun is not None:
                sums[i] = begun(i)
            sums[i] = term if sums[i] is None else sums[i] + term
    return sums


def padded_rows(low, mid, high, pick):
    margin, extent = low.shape[0], mid.shape[0]

    def rows(r):
        if r < margin:
            return pick(low, r)
        if r < margin + extent:
            return pick(mid, r - margin)
        return pick(high, r - margin - extent)

    return rows


def outer_rows(low, high, extent, pick):
    margin = low.shape[0]

    def rows(r):
        if r < margin:
            return pick(low, r)
        return pick(high, r - margin - extent) if r >= margin + extent else None

    return rows


def inner_rows(mid, margin, pick):
    return lambda r: pick(mid, r - margin) if margin <= r < margin + mid.shape[0] else None


def own_body(reverse, taps_ref, mid_ref, out_ref):
    extent, inner, width = mid_ref.shape
    margin = taps_ref.shape[0] // 2

    def tile(j, carry):
        lanes = lanes_at(j)
        taps = [taps_ref[k] for k in range(taps_ref.shape[0])]
        for at in range(0, inner, 8):
            pick = lambda ref, r: ref[r, at:at + 8, lanes]
            for i, value in enumerate(correlate(taps, inner_rows(mid_ref, margin, pick), extent, reverse)):
                out_ref[i, at:at + 8, lanes] = value
        return carry

    lax.fori_loop(0, width // LANES, tile, 0)


def own(taps, mid, reverse):
    (part,) = call(functools.partial(own_body, reverse), (taps, mid), [local(*mid.shape)])
    return part


def lanes_at(j):
    return pl.ds(pl.multiple_of(j * LANES, LANES), LANES)


def put(out_refs, i, at, lanes, value):
    mid_ref, first_ref, last_ref = out_refs
    extent, margin = mid_ref.shape[0], first_ref.shape[0]
    mid_ref[i, at, lanes] = value
    if i < margin:
        first_ref[i, at, lanes] = value
    if i >= extent - margin:
        last_ref[i - extent + margin, at, lanes] = value


def along_z(taps_ref, low_ref, mid_ref, high_ref, reverse, store):
    rows_y, width = mid_ref.shape[1], mid_ref.shape[2]

    def tile(j, carry):
        lanes = lanes_at(j)
        taps = [taps_ref[k] for k in range(taps_ref.shape[0])]
        for y in range(0, rows_y, 8):
            pick = lambda ref, r: ref[r, y:y + 8, lanes]
            extent = mid_ref.shape[0]
            begun = lambda i: mid_ref[i, y:y + 8, lanes]
            store(y, j, correlate(taps, outer_rows(low_ref, high_ref, extent, pick), extent, reverse, begun))
        return carry

    lax.fori_loop(0, width // LANES, tile, 0)


def depth_body(reverse, taps_ref, low_ref, mid_ref, high_ref, *out_refs):
    def store(y, j, sums):
        turned = jnp.swapaxes(jnp.stack(sums), 0, 1)
        for i in range(8):
            put(out_refs, y + i, slice(None), lanes_at(j), turned[i])

    along_z(taps_ref, low_ref, mid_ref, high_ref, reverse, store)


def depth(taps, low, mid, high, reverse, margin):
    nz, ny, nx = mid.shape
    shapes = [local(ny, nz, nx), local(margin, nz, nx), local(margin, nz, nx)]
    return call(functools.partial(depth_body, reverse), (taps, low, mid, high), shapes)


def plane_body(reverse, divide, taps_ref, low_ref, mid_ref, high_ref, *refs):
    view_ref, out_refs = (refs[0], refs[1:]) if divide else (None, refs)

    def tile(j, carry):
        lanes = lanes_at(j)
        taps = [taps_ref[k] for k in range(taps_ref.shape[0])]
        pick = lambda ref, r: ref[r, :, lanes]
        extent = mid_ref.shape[0]
        begun = lambda i: mid_ref[i, :, lanes]
        sums = correlate(taps, outer_rows(low_ref, high_ref, extent, pick), extent, reverse, begun)
        if divide:
            for i, value in enumerate(sums):
                put(out_refs, i, slice(None), lanes, view_ref[i, :, lanes] / value)
        else:
            for y in range(0, len(sums), 8):
                turned = jnp.swapaxes(jnp.stack(sums[y:y + 8]), 0, 1)
                for z in range(8):
                    put(out_refs, z, slice(y, y + 8), lanes, turned[z])
        return carry

    lax.fori_loop(0, mid_ref.shape[2] // LANES, tile, 0)


def plane(taps, low, mid, high, reverse, margin, view=None):
    ny, nz, nx = mid.shape
    outer, inner = (nz, ny) if view is None else (ny, nz)
    shapes = [local(outer, inner, nx), local(margin, inner, nx), local(margin, inner, nx)]
    operands = (taps, low, mid, high) + (() if view is None else (view,))
    return call(functools.partial(plane_body, reverse, view is not None), operands, shapes)


def deep_body(taps_ref, low_ref, mid_ref, high_ref, view_low_ref, view_ref, view_high_ref, *out_refs):
    extent = mid_ref.shape[0]

    def tile(j, carry):
        lanes = lanes_at(j)
        taps = [taps_ref[k] for k in range(taps_ref.shape[0])]
        pick = lambda ref, r: ref[r, :, lanes]
        wide = extent + len(taps) - 1
        sums = correlate(taps, padded_rows(low_ref, mid_ref, high_ref, pick), wide, False)
        seen = padded_rows(view_low_ref, view_ref, view_high_ref, pick)
        quotient = [seen(r) / value for r, value in enumerate(sums)]
        sums = correlate(taps, lambda r: quotient[r], extent, True)
        for y in range(0, extent, 8):
            turned = jnp.swapaxes(jnp.stack(sums[y:y + 8]), 0, 1)
            for z in range(8):
                put(out_refs, z, slice(y, y + 8), lanes, turned[z])
        return carry

    lax.fori_loop(0, mid_ref.shape[2] // LANES, tile, 0)


def deep(taps, halo, view, margin):
    ny, nz, nx = halo[1].shape
    shapes = [local(nz, ny, nx), local(margin, ny, nx), local(margin, ny, nx)]
    return call(deep_body, (taps, *halo, *view), shapes)


def clear_edges(wide_ref):
    blank = jnp.zeros((wide_ref.shape[0], LANES), jnp.float32)
    wide_ref[:, :LANES] = blank
    wide_ref[:, wide_ref.shape[1] - LANES:] = blank


def product(left, right):
    return jnp.dot(left, right, preferred_element_type=jnp.float32)


def along_x(wide_ref, band):
    high, low = halves(wide_ref[...])
    for j in range(wide_ref.shape[1] // LANES - 1):
        window = slice(j * LANES, (j + 2) * LANES)
        both = product(high[:, window], band)
        yield j, both[:, :LANES] + (both[:, LANES:] + product(low[:, window], band[:, :LANES]))


def put_ahead(wide_ref, band_ref, out_refs, ny):
    per_chunk = out_refs[0].shape[2] // LANES
    for j, value in along_x(wide_ref, band_ref[...]):
        chunk, inside = divmod(j, per_chunk)
        refs = out_refs[3 * chunk:3 * chunk + 3]
        lanes = slice(inside * LANES, (inside + 1) * LANES)
        for z in range(refs[0].shape[0]):
            put(refs, z, slice(None), lanes, value[z * ny:(z + 1) * ny])


def first_body(lateral_ref, estimate_ref, *refs):
    out_refs, (wide_ref, full_ref, band_ref) = refs[:-3], refs[-3:]
    nz, ny, nx = estimate_ref.shape
    count = lateral_ref.shape[2]
    fill_band(full_ref, normalized(lambda k: lateral_ref[0, 1, k], count), 1)
    split_band(full_ref, band_ref)
    clear_edges(wide_ref)
    wide_ref[:, SHIFT:SHIFT + nx] = estimate_ref[...].reshape(nz * ny, nx)
    put_ahead(wide_ref, band_ref, out_refs, ny)


def ahead_shapes(shape, margin):
    nz, ny, nx = shape
    part = nx // CHUNKS
    return [local(nz, ny, part), local(margin, ny, part), local(margin, ny, part)] * CHUNKS


def chunked(outs):
    return [tuple(outs[3 * c:3 * c + 3]) for c in range(CHUNKS)]


def first(lateral_kernel, estimate, margin):
    nz, ny, nx = estimate.shape
    shapes = ahead_shapes(estimate.shape, margin)
    outs = pl.pallas_call(
        first_body,
        out_shape=shapes,
        in_specs=[SMEM, VMEM],
        out_specs=[VMEM] * len(shapes),
        scratch_shapes=[
            local(nz * ny, nx + LANES),
            local(2 * LANES, LANES),
            pltpu.VMEM((2 * LANES, 2 * LANES), jnp.bfloat16),
        ],
        compiler_params=LIMIT,
        name="first",
    )(lateral_kernel, pltpu.with_memory_space_constraint(estimate, pltpu.VMEM))
    return chunked(outs)


def update_body(last, taps_ref, band_ref, estimate_ref, *refs):
    halo_refs, refs = refs[:3 * CHUNKS], refs[3 * CHUNKS:]
    refs, (wide_ref, mixed_ref) = refs[:-2], refs[-2:]
    if last:
        (out_ref,) = refs
    else:
        next_ref, out_ref, *ahead_refs = refs
    nz, ny, nx = estimate_ref.shape
    per_chunk = nx // CHUNKS // LANES
    for c in range(CHUNKS):
        def store(y, j, sums):
            for z, value in enumerate(sums):
                mixed_ref[z * ny + y:z * ny + y + 8, lanes_at(j + c * per_chunk)] = value

        along_z(taps_ref, *halo_refs[3 * c:3 * c + 3], True, store)
    clear_edges(wide_ref)
    wide_ref[:, SHIFT:SHIFT + nx] = mixed_ref[...]
    for j, value in along_x(wide_ref, band_ref[...]):
        at = slice(j * LANES, (j + 1) * LANES)
        out_ref[:, :, at] = estimate_ref[:, :, at] * value.reshape(nz, ny, LANES)
    if not last:
        wide_ref[:, SHIFT:SHIFT + nx] = out_ref[...].reshape(nz * ny, nx)
        put_ahead(wide_ref, next_ref, ahead_refs, ny)


def update(taps, halos, band, estimate, band_next=None):
    nz, ny, nx = estimate.shape
    last = band_next is None
    operands = (taps, band, estimate) + sum(halos, ()) + (() if last else (band_next,))
    shapes = [local(nz, ny, nx)]
    if last:
        shapes = [jax.ShapeDtypeStruct((nz, ny, nx), jnp.float32)]
    else:
        shapes += ahead_shapes(estimate.shape, taps.shape[0] // 2)
    scratch = [local(nz * ny, nx + LANES), local(nz * ny, nx)]
    outs = call(functools.partial(update_body, last), operands, shapes, scratch)
    return outs[0], (None if last else chunked(outs[1:]))


def exchange(parts, axis):
    block, first_rows, last_rows = parts
    count = lax.axis_size(axis)
    forward = [(i, i + 1) for i in range(count - 1)]
    backward = [(target, source) for source, target in forward]
    low = lax.ppermute(last_rows, axis, forward)
    high = lax.ppermute(first_rows, axis, backward)
    return low, block, high


def pack_body(view_ref, out_ref):
    nz, nx, ny = view_ref.shape
    group = LANES // nz
    slot = lax.broadcasted_iota(jnp.int32, (8, LANES), 1) // group

    def tile(step, carry):
        t, at = step // (nx // 8), pl.ds(pl.multiple_of(step % (nx // 8) * 8, 8), 8)
        parts = [view_ref[z, at, lanes_at(t)] for z in range(nz)]
        span = nz // 2
        while span:
            odd = (slot & span) != 0
            for z in range(nz):
                if not z & span:
                    one, two = parts[z], parts[z + span]
                    parts[z] = jnp.where(odd, pltpu.roll(two, group * span, 1), one)
                    parts[z + span] = jnp.where(odd, two, pltpu.roll(one, LANES - group * span, 1))
            span //= 2
        for z in range(nz):
            out_ref[t * nz + z, at, :] = parts[z]
        return carry

    lax.fori_loop(0, ny // LANES * (nx // 8), tile, 0, unroll=True)


def unpack_body(arrived_ref, *out_refs):
    count, nx = arrived_ref.shape[0], arrived_ref.shape[1]
    nz, ny = out_refs[0].shape[1], out_refs[0].shape[0]
    flat = arrived_ref[...].reshape(count * nx, LANES)
    for j in range(count * nx // LANES):
        lanes = slice(j * LANES, (j + 1) * LANES)
        turned = jnp.swapaxes(flat[lanes].T.reshape(nz, ny, LANES), 0, 1)
        for y in range(ny):
            put(out_refs, y, slice(None), lanes, turned[y])


def halo(taps, parts, axis, reverse):
    low, block, high = exchange(parts, axis)
    return low, own(taps, block, reverse), high


def reframe(view, margin):
    nz, nx, ny = view.shape
    count = lax.axis_size("row")
    rows = ny // count
    (pieces,) = call(pack_body, (view,), [local(count, nx, rows * nz)])
    arrived = lax.all_to_all(pieces, "row", 0, 0, tiled=True)
    shapes = [local(rows, nz, count * nx), local(margin, nz, count * nx), local(margin, nz, count * nx)]
    return call(unpack_body, (arrived,), shapes)


def per_device(view_a, view_b, estimate, axial_kernel, lateral_kernel):
    margin_a, margin = axial_kernel.shape[1] // 2, lateral_kernel.shape[2] // 2
    seen_a = jnp.swapaxes(view_a, 0, 1)
    seen_b = exchange(reframe(view_b, margin), "row")
    ytaps, ztaps, bands = prepare(axial_kernel, lateral_kernel)
    (ahead,) = first(lateral_kernel, estimate, margin)
    steps = 2 * ITERS
    for step in range(steps):
        v = step % 2
        yt, zt = ytaps[v], ztaps[v]
        ahead = depth(zt, *halo(zt, ahead, "col", False), False, 2 * margin if v else margin_a)
        if v:
            ahead = deep(yt, exchange(ahead, "row"), seen_b, margin)
        else:
            ahead = plane(yt, *halo(yt, ahead, "row", False), False, margin_a, seen_a)
            ahead = plane(yt, *halo(yt, ahead, "row", True), True, margin)
        outer = halo(zt, ahead, "col", True)
        if step == steps - 1:
            estimate, _ = update(zt, [outer], bands[v][1], estimate)
        else:
            estimate, (ahead,) = update(zt, [outer], bands[v][1], estimate, bands[1 - v][0])
    return estimate


def solution(mesh):
    in_specs = (P("col", "row", None), P("col", "row", None), P("col", "row", None), P(), P())
    out_specs = P("col", "row", None)
    return jax.shard_map(per_device, mesh=mesh, in_specs=in_specs, out_specs=out_specs, check_vma=False)
```

```python
import functools
import jax
import jax.numpy as jnp
from jax import lax
from jax.experimental import pallas as pl
from jax.experimental.pallas import tpu as pltpu
from jax.sharding import PartitionSpec as P

ITERS = 2
LANES = 128
SHIFT = 64
CHUNKS = 1
CHUNK_LIMIT = 8 * 2**20
VMEM = pl.BlockSpec(memory_space=pltpu.VMEM)
LIMIT = pltpu.CompilerParams(vmem_limit_bytes=CHUNK_LIMIT)
SMEM = pl.BlockSpec(memory_space=pltpu.SMEM)


def splat(value):
    return jnp.full((8, LANES), value, jnp.float32)


def normalized(read, count):
    taps = [read(k) for k in range(count)]
    total = taps[0]
    for tap in taps[1:]:
        total = total + tap
    total = splat(total)
    return [splat(tap) / total for tap in taps]


def fill_band(band_ref, taps, sign):
    half = len(taps) // 2
    lane = lax.broadcasted_iota(jnp.int32, (8, LANES), 1)
    sub = lax.broadcasted_iota(jnp.int32, (8, LANES), 0)

    def fill(step, carry):
        distance = sign * (sub + step * 8 - lane - SHIFT)
        value = jnp.zeros((8, LANES), jnp.float32)
        for k, tap in enumerate(taps):
            value = jnp.where(distance == k - half, tap, value)
        band_ref[pl.ds(pl.multiple_of(step * 8, 8), 8), :] = value
        return carry

    start, stop = (SHIFT - 7 - half) // 8, (SHIFT + LANES - 1 + half) // 8 + 1
    band_ref[:8 * start, :] = jnp.zeros((8 * start, LANES), jnp.float32)
    band_ref[8 * stop:, :] = jnp.zeros((2 * LANES - 8 * stop, LANES), jnp.float32)
    lax.fori_loop(start, stop, fill, 0, unroll=True)


def halves(value):
    high = value.astype(jnp.bfloat16)
    return high, (value - high.astype(jnp.float32)).astype(jnp.bfloat16)


def split_band(wide_ref, out_ref):
    out_ref[:, :LANES], out_ref[:, LANES:] = halves(wide_ref[...])


def prepare_body(axial_ref, lateral_ref, ya_ref, yb_ref, za_ref, zb_ref, *band_refs):
    band_refs, full_ref = band_refs[:-1], band_refs[-1]
    axial, lateral = axial_ref.shape[1], lateral_ref.shape[2]
    rows = (
        (ya_ref, lambda k: axial_ref[0, k], axial),
        (yb_ref, lambda k: lateral_ref[1, 1, k], lateral),
        (za_ref, lambda k: lateral_ref[0, 0, k], lateral),
        (zb_ref, lambda k: lateral_ref[1, 0, k], lateral),
    )
    for target, read, count in rows:
        for k, tap in enumerate(normalized(read, count)):
            target[k] = tap
    xa = normalized(lambda k: lateral_ref[0, 1, k], lateral)
    xb = normalized(lambda k: axial_ref[1, k], axial)
    for taps, refs in ((xa, band_refs[:2]), (xb, band_refs[2:])):
        for ref, sign in zip(refs, (1, -1)):
            fill_band(full_ref, taps, sign)
            split_band(full_ref, ref)


def local(*shape):
    return pltpu.VMEM(shape, jnp.float32)


def call(body, operands, shapes, scratch=()):
    operands = [pltpu.with_memory_space_constraint(operand, pltpu.VMEM) for operand in operands]
    return pl.pallas_call(
        body,
        out_shape=shapes,
        in_specs=[VMEM] * len(operands),
        out_specs=[VMEM] * len(shapes),
        scratch_shapes=scratch,
        compiler_params=LIMIT,
    )(*operands)


def prepare(axial_kernel, lateral_kernel):
    axial, lateral = axial_kernel.shape[1], lateral_kernel.shape[2]
    shapes = [local(count, 8, LANES) for count in (axial, lateral, lateral, lateral)]
    shapes += [pltpu.VMEM((2 * LANES, 2 * LANES), jnp.bfloat16)] * 4
    outs = pl.pallas_call(
        prepare_body,
        out_shape=shapes,
        in_specs=[SMEM, SMEM],
        out_specs=[VMEM] * len(shapes),
        scratch_shapes=[local(2 * LANES, LANES)],
        compiler_params=LIMIT,
        name="prepare",
    )(axial_kernel, lateral_kernel)
    return outs[:2], outs[2:4], (outs[4:6], outs[6:8])


def correlate(taps, rows, extent, reverse, begun=None):
    count = len(taps)
    sums = [None] * extent
    for r in range(extent + count - 1):
        value = rows(r)
        if value is None:
            continue
        for i in range(max(0, r - count + 1), min(extent, r + 1)):
            k = r - i
            term = taps[count - 1 - k if reverse else k] * value
            if sums[i] is None and begun is not None:
                sums[i] = begun(i)
            sums[i] = term if sums[i] is None else sums[i] + term
    return [begun(i) if value is None else value for i, value in enumerate(sums)]


def padded_rows(low, mid, high, pick):
    margin, extent = low.shape[0], mid.shape[0]

    def rows(r):
        if r < margin:
            return pick(low, r)
        if r < margin + extent:
            return pick(mid, r - margin)
        return pick(high, r - margin - extent)

    return rows


def outer_rows(low, high, extent, pick):
    margin = low.shape[0]

    def rows(r):
        if r < margin:
            return pick(low, r)
        return pick(high, r - margin - extent) if r >= margin + extent else None

    return rows


def inner_rows(mid, margin, pick):
    return lambda r: pick(mid, r - margin) if margin <= r < margin + mid.shape[0] else None


def own_body(reverse, margin, taps_ref, mid_ref, out_ref):
    extent, (_, inner, width) = out_ref.shape[0], mid_ref.shape

    def tile(j, carry):
        lanes = lanes_at(j)
        taps = [taps_ref[k] for k in range(taps_ref.shape[0])]
        for at in range(0, inner, 8):
            pick = lambda ref, r: ref[r, at:at + 8, lanes]
            for i, value in enumerate(correlate(taps, inner_rows(mid_ref, margin, pick), extent, reverse)):
                out_ref[i, at:at + 8, lanes] = value
        return carry

    lax.fori_loop(0, width // LANES, tile, 0)


def own(taps, mid, margin, reverse):
    extent = mid.shape[0] + 2 * margin - taps.shape[0] + 1
    shapes = [local(extent, *mid.shape[1:])]
    (part,) = call(functools.partial(own_body, reverse, margin), (taps, mid), shapes)
    return part


def lanes_at(j):
    return pl.ds(pl.multiple_of(j * LANES, LANES), LANES)


def put(out_refs, i, at, lanes, value):
    mid_ref, first_ref, last_ref = out_refs
    extent, margin = mid_ref.shape[0], first_ref.shape[0]
    mid_ref[i, at, lanes] = value
    if i < margin:
        first_ref[i, at, lanes] = value
    if i >= extent - margin:
        last_ref[i - extent + margin, at, lanes] = value


def along_z(taps_ref, low_ref, mid_ref, high_ref, reverse, store):
    rows_y, width = mid_ref.shape[1], mid_ref.shape[2]

    def tile(j, carry):
        lanes = lanes_at(j)
        taps = [taps_ref[k] for k in range(taps_ref.shape[0])]
        for y in range(0, rows_y, 8):
            pick = lambda ref, r: ref[r, y:y + 8, lanes]
            extent = mid_ref.shape[0]
            begun = lambda i: mid_ref[i, y:y + 8, lanes]
            store(y, j, correlate(taps, outer_rows(low_ref, high_ref, extent, pick), extent, reverse, begun))
        return carry

    lax.fori_loop(0, width // LANES, tile, 0)


def depth_body(reverse, taps_ref, low_ref, mid_ref, high_ref, *out_refs):
    def store(y, j, sums):
        turned = jnp.swapaxes(jnp.stack(sums), 0, 1)
        for i in range(8):
            put(out_refs, y + i, slice(None), lanes_at(j), turned[i])

    along_z(taps_ref, low_ref, mid_ref, high_ref, reverse, store)


def depth(taps, low, mid, high, reverse, margin):
    nz, ny, nx = mid.shape
    shapes = [local(ny, nz, nx), local(margin, nz, nx), local(margin, nz, nx)]
    return call(functools.partial(depth_body, reverse), (taps, low, mid, high), shapes)


def plane_body(reverse, divide, taps_ref, low_ref, mid_ref, high_ref, *refs):
    view_ref, out_refs = (refs[0], refs[1:]) if divide else (None, refs)

    def tile(j, carry):
        lanes = lanes_at(j)
        taps = [taps_ref[k] for k in range(taps_ref.shape[0])]
        pick = lambda ref, r: ref[r, :, lanes]
        extent = mid_ref.shape[0]
        begun = lambda i: mid_ref[i, :, lanes]
        sums = correlate(taps, outer_rows(low_ref, high_ref, extent, pick), extent, reverse, begun)
        if divide:
            for i, value in enumerate(sums):
                put(out_refs, i, slice(None), lanes, view_ref[i, :, lanes] / value)
        else:
            for y in range(0, len(sums), 8):
                turned = jnp.swapaxes(jnp.stack(sums[y:y + 8]), 0, 1)
                for z in range(8):
                    put(out_refs, z, slice(y, y + 8), lanes, turned[z])
        return carry

    lax.fori_loop(0, mid_ref.shape[2] // LANES, tile, 0)


def plane(taps, low, mid, high, reverse, margin, view=None):
    ny, nz, nx = mid.shape
    outer, inner = (nz, ny) if view is None else (ny, nz)
    shapes = [local(outer, inner, nx), local(margin, inner, nx), local(margin, inner, nx)]
    operands = (taps, low, mid, high) + (() if view is None else (view,))
    return call(functools.partial(plane_body, reverse, view is not None), operands, shapes)


def deep_body(taps_ref, low_ref, mid_ref, high_ref, view_low_ref, view_ref, view_high_ref, *out_refs):
    extent = view_ref.shape[0]

    def tile(j, carry):
        lanes = lanes_at(j)
        taps = [taps_ref[k] for k in range(taps_ref.shape[0])]
        pick = lambda ref, r: ref[r, :, lanes]
        wide = extent + len(taps) - 1
        begun = lambda i: mid_ref[i, :, lanes]
        sums = correlate(taps, outer_rows(low_ref, high_ref, extent, pick), wide, False, begun)
        seen = padded_rows(view_low_ref, view_ref, view_high_ref, pick)
        quotient = [seen(r) / value for r, value in enumerate(sums)]
        sums = correlate(taps, lambda r: quotient[r], extent, True)
        for y in range(0, extent, 8):
            turned = jnp.swapaxes(jnp.stack(sums[y:y + 8]), 0, 1)
            for z in range(8):
                put(out_refs, z, slice(y, y + 8), lanes, turned[z])
        return carry

    lax.fori_loop(0, mid_ref.shape[2] // LANES, tile, 0)


def deep(taps, outer, view, margin):
    ny, nz, nx = view[1].shape
    shapes = [local(nz, ny, nx), local(margin, ny, nx), local(margin, ny, nx)]
    return call(deep_body, (taps, *outer, *view), shapes)


def clear_edges(wide_ref):
    blank = jnp.zeros((wide_ref.shape[0], LANES), jnp.float32)
    wide_ref[:, :LANES] = blank
    wide_ref[:, wide_ref.shape[1] - LANES:] = blank


def product(left, right):
    return jnp.dot(left, right, preferred_element_type=jnp.float32)


def along_x(wide_ref, band):
    high, low = halves(wide_ref[...])
    for j in range(wide_ref.shape[1] // LANES - 1):
        window = slice(j * LANES, (j + 2) * LANES)
        both = product(high[:, window], band)
        yield j, both[:, :LANES] + (both[:, LANES:] + product(low[:, window], band[:, :LANES]))


def put_ahead(wide_ref, band_ref, out_refs, ny):
    per_chunk = out_refs[0].shape[2] // LANES
    for j, value in along_x(wide_ref, band_ref[...]):
        chunk, inside = divmod(j, per_chunk)
        refs = out_refs[3 * chunk:3 * chunk + 3]
        lanes = slice(inside * LANES, (inside + 1) * LANES)
        for z in range(refs[0].shape[0]):
            put(refs, z, slice(None), lanes, value[z * ny:(z + 1) * ny])


def first_body(lateral_ref, estimate_ref, *refs):
    out_refs, (wide_ref, full_ref, band_ref, held_ref, sem) = refs[:-5], refs[-5:]
    nz, ny, nx = estimate_ref.shape
    count = lateral_ref.shape[2]
    copy = pltpu.make_async_copy(estimate_ref, held_ref, sem)
    copy.start()
    fill_band(full_ref, normalized(lambda k: lateral_ref[0, 1, k], count), 1)
    split_band(full_ref, band_ref)
    clear_edges(wide_ref)
    copy.wait()
    wide_ref[:, SHIFT:SHIFT + nx] = held_ref[...].reshape(nz * ny, nx)
    put_ahead(wide_ref, band_ref, out_refs, ny)


def ahead_shapes(shape, margin):
    nz, ny, nx = shape
    part = nx // CHUNKS
    return [local(nz, ny, part), local(margin, ny, part), local(margin, ny, part)] * CHUNKS


def chunked(outs):
    return [tuple(outs[3 * c:3 * c + 3]) for c in range(CHUNKS)]


def first(lateral_kernel, estimate, margin):
    nz, ny, nx = estimate.shape
    shapes = ahead_shapes(estimate.shape, margin)
    outs = pl.pallas_call(
        first_body,
        out_shape=shapes,
        in_specs=[SMEM, pl.BlockSpec(memory_space=pltpu.HBM)],
        out_specs=[VMEM] * len(shapes),
        scratch_shapes=[
            local(nz * ny, nx + LANES),
            local(2 * LANES, LANES),
            pltpu.VMEM((2 * LANES, 2 * LANES), jnp.bfloat16),
            local(nz, ny, nx),
            pltpu.SemaphoreType.DMA(()),
        ],
        compiler_params=LIMIT,
        name="first",
    )(lateral_kernel, pltpu.with_memory_space_constraint(estimate, pltpu.HBM))
    return chunked(outs)


def update_body(last, taps_ref, band_ref, estimate_ref, *refs):
    halo_refs, refs = refs[:3 * CHUNKS], refs[3 * CHUNKS:]
    refs, (wide_ref, mixed_ref) = refs[:-2], refs[-2:]
    if last:
        (out_ref,) = refs
    else:
        next_ref, out_ref, *ahead_refs = refs
    nz, ny, nx = estimate_ref.shape
    per_chunk = nx // CHUNKS // LANES
    for c in range(CHUNKS):
        def store(y, j, sums):
            for z, value in enumerate(sums):
                mixed_ref[z * ny + y:z * ny + y + 8, lanes_at(j + c * per_chunk)] = value

        along_z(taps_ref, *halo_refs[3 * c:3 * c + 3], True, store)
    clear_edges(wide_ref)
    wide_ref[:, SHIFT:SHIFT + nx] = mixed_ref[...]
    for j, value in along_x(wide_ref, band_ref[...]):
        at = slice(j * LANES, (j + 1) * LANES)
        out_ref[:, :, at] = estimate_ref[:, :, at] * value.reshape(nz, ny, LANES)
    if not last:
        wide_ref[:, SHIFT:SHIFT + nx] = out_ref[...].reshape(nz * ny, nx)
        put_ahead(wide_ref, next_ref, ahead_refs, ny)


def update(taps, halos, band, estimate, band_next=None):
    nz, ny, nx = estimate.shape
    last = band_next is None
    operands = (taps, band, estimate) + sum(halos, ()) + (() if last else (band_next,))
    shapes = [local(nz, ny, nx)]
    if last:
        shapes = [jax.ShapeDtypeStruct((nz, ny, nx), jnp.float32)]
    else:
        shapes += ahead_shapes(estimate.shape, taps.shape[0] // 2)
    scratch = [local(nz * ny, nx + LANES), local(nz * ny, nx)]
    outs = call(functools.partial(update_body, last), operands, shapes, scratch)
    return outs[0], (None if last else chunked(outs[1:]))


def exchange(parts, axis):
    block, first_rows, last_rows = parts
    count = lax.axis_size(axis)
    forward = [(i, i + 1) for i in range(count - 1)]
    backward = [(target, source) for source, target in forward]
    low = lax.ppermute(last_rows, axis, forward)
    high = lax.ppermute(first_rows, axis, backward)
    return low, block, high


def pack_body(view_ref, out_ref):
    nz, nx, ny = view_ref.shape
    group = LANES // nz
    slot = lax.broadcasted_iota(jnp.int32, (8, LANES), 1) // group

    def tile(step, carry):
        t, at = step // (nx // 8), pl.ds(pl.multiple_of(step % (nx // 8) * 8, 8), 8)
        parts = [view_ref[z, at, lanes_at(t)] for z in range(nz)]
        span = nz // 2
        while span:
            odd = (slot & span) != 0
            for z in range(nz):
                if not z & span:
                    one, two = parts[z], parts[z + span]
                    parts[z] = jnp.where(odd, pltpu.roll(two, group * span, 1), one)
                    parts[z + span] = jnp.where(odd, two, pltpu.roll(one, LANES - group * span, 1))
            span //= 2
        for z in range(nz):
            out_ref[t * nz + z, at, :] = parts[z]
        return carry

    lax.fori_loop(0, ny // LANES * (nx // 8), tile, 0, unroll=True)


def unpack_body(arrived_ref, *out_refs):
    count, nx = arrived_ref.shape[0], arrived_ref.shape[1]
    nz, ny = out_refs[0].shape[1], out_refs[0].shape[0]
    flat = arrived_ref[...].reshape(count * nx, LANES)
    for j in range(count * nx // LANES):
        lanes = slice(j * LANES, (j + 1) * LANES)
        turned = jnp.swapaxes(flat[lanes].T.reshape(nz, ny, LANES), 0, 1)
        for y in range(ny):
            put(out_refs, y, slice(None), lanes, turned[y])


def halo(taps, parts, axis, reverse):
    low, block, high = exchange(parts, axis)
    return low, own(taps, block, low.shape[0], reverse), high


def reframe(view, margin):
    nz, nx, ny = view.shape
    count = lax.axis_size("row")
    rows = ny // count
    (pieces,) = call(pack_body, (view,), [local(count, nx, rows * nz)])
    arrived = lax.all_to_all(pieces, "row", 0, 0, tiled=True)
    shapes = [local(rows, nz, count * nx), local(margin, nz, count * nx), local(margin, nz, count * nx)]
    return call(unpack_body, (arrived,), shapes)


def per_device(view_a, view_b, estimate, axial_kernel, lateral_kernel):
    margin_a, margin = axial_kernel.shape[1] // 2, lateral_kernel.shape[2] // 2
    seen_a = jnp.swapaxes(view_a, 0, 1)
    seen_b = exchange(reframe(view_b, margin), "row")
    ytaps, ztaps, bands = prepare(axial_kernel, lateral_kernel)
    (ahead,) = first(lateral_kernel, estimate, margin)
    steps = 2 * ITERS
    for step in range(steps):
        v = step % 2
        yt, zt = ytaps[v], ztaps[v]
        ahead = depth(zt, *halo(zt, ahead, "col", False), False, 2 * margin if v else margin_a)
        if v:
            ahead = deep(yt, halo(yt, ahead, "row", False), seen_b, margin)
        else:
            ahead = plane(yt, *halo(yt, ahead, "row", False), False, margin_a, seen_a)
            ahead = plane(yt, *halo(yt, ahead, "row", True), True, margin)
        outer = halo(zt, ahead, "col", True)
        if step == steps - 1:
            estimate, _ = update(zt, [outer], bands[v][1], estimate)
        else:
            estimate, (ahead,) = update(zt, [outer], bands[v][1], estimate, bands[1 - v][0])
    return estimate


def solution(mesh):
    in_specs = (P("col", "row", None), P("col", "row", None), P("col", "row", None), P(), P())
    out_specs = P("col", "row", None)
    return jax.shard_map(per_device, mesh=mesh, in_specs=in_specs, out_specs=out_specs, check_vma=False)
```

```python
import functools
import jax
import jax.numpy as jnp
from jax import lax
from jax.experimental import pallas as pl
from jax.experimental.pallas import tpu as pltpu
from jax.sharding import PartitionSpec as P

ITERS = 2
LANES = 128
SHIFT = 64
CHUNKS = 1
CHUNK_LIMIT = 8 * 2**20
VMEM = pl.BlockSpec(memory_space=pltpu.VMEM)
LIMIT = pltpu.CompilerParams(vmem_limit_bytes=CHUNK_LIMIT)
SMEM = pl.BlockSpec(memory_space=pltpu.SMEM)


def splat(value):
    return jnp.full((8, LANES), value, jnp.float32)


def normalized(read, count):
    taps = [read(k) for k in range(count)]
    total = taps[0]
    for tap in taps[1:]:
        total = total + tap
    total = splat(total)
    return [splat(tap) / total for tap in taps]


def fill_band(band_ref, taps, sign):
    half = len(taps) // 2
    lane = lax.broadcasted_iota(jnp.int32, (8, LANES), 1)
    sub = lax.broadcasted_iota(jnp.int32, (8, LANES), 0)

    def fill(step, carry):
        distance = sign * (sub + step * 8 - lane - SHIFT)
        value = jnp.zeros((8, LANES), jnp.float32)
        for k, tap in enumerate(taps):
            value = jnp.where(distance == k - half, tap, value)
        band_ref[pl.ds(pl.multiple_of(step * 8, 8), 8), :] = value
        return carry

    start, stop = (SHIFT - 7 - half) // 8, (SHIFT + LANES - 1 + half) // 8 + 1
    band_ref[:8 * start, :] = jnp.zeros((8 * start, LANES), jnp.float32)
    band_ref[8 * stop:, :] = jnp.zeros((2 * LANES - 8 * stop, LANES), jnp.float32)
    lax.fori_loop(start, stop, fill, 0, unroll=True)


def halves(value):
    high = value.astype(jnp.bfloat16)
    return high, (value - high.astype(jnp.float32)).astype(jnp.bfloat16)


def split_band(wide_ref, out_ref):
    out_ref[:, :LANES], out_ref[:, LANES:] = halves(wide_ref[...])


def prepare_body(axial_ref, lateral_ref, ya_ref, yb_ref, za_ref, zb_ref, *band_refs):
    band_refs, full_ref = band_refs[:-1], band_refs[-1]
    axial, lateral = axial_ref.shape[1], lateral_ref.shape[2]
    rows = (
        (ya_ref, lambda k: axial_ref[0, k], axial),
        (yb_ref, lambda k: lateral_ref[1, 1, k], lateral),
        (za_ref, lambda k: lateral_ref[0, 0, k], lateral),
        (zb_ref, lambda k: lateral_ref[1, 0, k], lateral),
    )
    for target, read, count in rows:
        for k, tap in enumerate(normalized(read, count)):
            target[k] = tap
    xa = normalized(lambda k: lateral_ref[0, 1, k], lateral)
    xb = normalized(lambda k: axial_ref[1, k], axial)
    for taps, refs in ((xa, band_refs[:2]), (xb, band_refs[2:])):
        for ref, sign in zip(refs, (1, -1)):
            fill_band(full_ref, taps, sign)
            split_band(full_ref, ref)


def local(*shape):
    return pltpu.VMEM(shape, jnp.float32)


def call(body, operands, shapes, scratch=()):
    operands = [pltpu.with_memory_space_constraint(operand, pltpu.VMEM) for operand in operands]
    return pl.pallas_call(
        body,
        out_shape=shapes,
        in_specs=[VMEM] * len(operands),
        out_specs=[VMEM] * len(shapes),
        scratch_shapes=scratch,
        compiler_params=LIMIT,
    )(*operands)


def prepare(axial_kernel, lateral_kernel):
    axial, lateral = axial_kernel.shape[1], lateral_kernel.shape[2]
    shapes = [local(count, 8, LANES) for count in (axial, lateral, lateral, lateral)]
    shapes += [pltpu.VMEM((2 * LANES, 2 * LANES), jnp.bfloat16)] * 4
    outs = pl.pallas_call(
        prepare_body,
        out_shape=shapes,
        in_specs=[SMEM, SMEM],
        out_specs=[VMEM] * len(shapes),
        scratch_shapes=[local(2 * LANES, LANES)],
        compiler_params=LIMIT,
        name="prepare",
    )(axial_kernel, lateral_kernel)
    return outs[:2], outs[2:4], (outs[4:6], outs[6:8])


def correlate(taps, rows, extent, reverse, begun=None):
    count = len(taps)
    sums = [None] * extent
    for r in range(extent + count - 1):
        value = rows(r)
        if value is None:
            continue
        for i in range(max(0, r - count + 1), min(extent, r + 1)):
            k = r - i
            term = taps[count - 1 - k if reverse else k] * value
            if sums[i] is None and begun is not None:
                sums[i] = begun(i)
            sums[i] = term if sums[i] is None else sums[i] + term
    return [begun(i) if value is None else value for i, value in enumerate(sums)]


def padded_rows(low, mid, high, pick):
    margin, extent = low.shape[0], mid.shape[0]

    def rows(r):
        if r < margin:
            return pick(low, r)
        if r < margin + extent:
            return pick(mid, r - margin)
        return pick(high, r - margin - extent)

    return rows


def outer_rows(low, high, extent, pick):
    margin = low.shape[0]

    def rows(r):
        if r < margin:
            return pick(low, r)
        return pick(high, r - margin - extent) if r >= margin + extent else None

    return rows


def inner_rows(mid, margin, pick):
    return lambda r: pick(mid, r - margin) if margin <= r < margin + mid.shape[0] else None


def own_body(reverse, margin, taps_ref, mid_ref, out_ref):
    extent, (_, inner, width) = out_ref.shape[0], mid_ref.shape

    def tile(j, carry):
        lanes = lanes_at(j)
        taps = [taps_ref[k] for k in range(taps_ref.shape[0])]
        for at in range(0, inner, 8):
            pick = lambda ref, r: ref[r, at:at + 8, lanes]
            for i, value in enumerate(correlate(taps, inner_rows(mid_ref, margin, pick), extent, reverse)):
                out_ref[i, at:at + 8, lanes] = value
        return carry

    lax.fori_loop(0, width // LANES, tile, 0, unroll=2)


def own(taps, mid, margin, reverse):
    extent = mid.shape[0] + 2 * margin - taps.shape[0] + 1
    shapes = [local(extent, *mid.shape[1:])]
    (part,) = call(functools.partial(own_body, reverse, margin), (taps, mid), shapes)
    return part


def lanes_at(j):
    return pl.ds(pl.multiple_of(j * LANES, LANES), LANES)


def put(out_refs, i, at, lanes, value):
    mid_ref, first_ref, last_ref = out_refs
    extent, margin = mid_ref.shape[0], first_ref.shape[0]
    mid_ref[i, at, lanes] = value
    if i < margin:
        first_ref[i, at, lanes] = value
    if i >= extent - margin:
        last_ref[i - extent + margin, at, lanes] = value


def along_z(taps_ref, low_ref, mid_ref, high_ref, reverse, store):
    rows_y, width = mid_ref.shape[1], mid_ref.shape[2]

    def tile(j, carry):
        lanes = lanes_at(j)
        taps = [taps_ref[k] for k in range(taps_ref.shape[0])]
        for y in range(0, rows_y, 8):
            pick = lambda ref, r: ref[r, y:y + 8, lanes]
            extent = mid_ref.shape[0]
            begun = lambda i: mid_ref[i, y:y + 8, lanes]
            store(y, j, correlate(taps, outer_rows(low_ref, high_ref, extent, pick), extent, reverse, begun))
        return carry

    lax.fori_loop(0, width // LANES, tile, 0, unroll=2)


def depth_body(reverse, taps_ref, low_ref, mid_ref, high_ref, *out_refs):
    def store(y, j, sums):
        turned = jnp.swapaxes(jnp.stack(sums), 0, 1)
        for i in range(8):
            put(out_refs, y + i, slice(None), lanes_at(j), turned[i])

    along_z(taps_ref, low_ref, mid_ref, high_ref, reverse, store)


def depth(taps, low, mid, high, reverse, margin):
    nz, ny, nx = mid.shape
    shapes = [local(ny, nz, nx), local(margin, nz, nx), local(margin, nz, nx)]
    return call(functools.partial(depth_body, reverse), (taps, low, mid, high), shapes)


def plane_body(reverse, divide, taps_ref, low_ref, mid_ref, high_ref, *refs):
    view_ref, out_refs = (refs[0], refs[1:]) if divide else (None, refs)

    def tile(j, carry):
        lanes = lanes_at(j)
        taps = [taps_ref[k] for k in range(taps_ref.shape[0])]
        pick = lambda ref, r: ref[r, :, lanes]
        extent = mid_ref.shape[0]
        begun = lambda i: mid_ref[i, :, lanes]
        sums = correlate(taps, outer_rows(low_ref, high_ref, extent, pick), extent, reverse, begun)
        if divide:
            for i, value in enumerate(sums):
                put(out_refs, i, slice(None), lanes, view_ref[i, :, lanes] / value)
        else:
            for y in range(0, len(sums), 8):
                turned = jnp.swapaxes(jnp.stack(sums[y:y + 8]), 0, 1)
                for z in range(8):
                    put(out_refs, z, slice(y, y + 8), lanes, turned[z])
        return carry

    lax.fori_loop(0, mid_ref.shape[2] // LANES, tile, 0)


def plane(taps, low, mid, high, reverse, margin, view=None):
    ny, nz, nx = mid.shape
    outer, inner = (nz, ny) if view is None else (ny, nz)
    shapes = [local(outer, inner, nx), local(margin, inner, nx), local(margin, inner, nx)]
    operands = (taps, low, mid, high) + (() if view is None else (view,))
    return call(functools.partial(plane_body, reverse, view is not None), operands, shapes)


def deep_body(taps_ref, low_ref, mid_ref, high_ref, view_low_ref, view_ref, view_high_ref, *out_refs):
    extent = view_ref.shape[0]

    def tile(j, carry):
        lanes = lanes_at(j)
        taps = [taps_ref[k] for k in range(taps_ref.shape[0])]
        pick = lambda ref, r: ref[r, :, lanes]
        wide = extent + len(taps) - 1
        begun = lambda i: mid_ref[i, :, lanes]
        sums = correlate(taps, outer_rows(low_ref, high_ref, extent, pick), wide, False, begun)
        seen = padded_rows(view_low_ref, view_ref, view_high_ref, pick)
        quotient = [seen(r) / value for r, value in enumerate(sums)]
        sums = correlate(taps, lambda r: quotient[r], extent, True)
        for y in range(0, extent, 8):
            turned = jnp.swapaxes(jnp.stack(sums[y:y + 8]), 0, 1)
            for z in range(8):
                put(out_refs, z, slice(y, y + 8), lanes, turned[z])
        return carry

    lax.fori_loop(0, mid_ref.shape[2] // LANES, tile, 0)


def deep(taps, outer, view, margin):
    ny, nz, nx = view[1].shape
    shapes = [local(nz, ny, nx), local(margin, ny, nx), local(margin, ny, nx)]
    return call(deep_body, (taps, *outer, *view), shapes)


def clear_edges(wide_ref):
    blank = jnp.zeros((wide_ref.shape[0], LANES), jnp.float32)
    wide_ref[:, :LANES] = blank
    wide_ref[:, wide_ref.shape[1] - LANES:] = blank


def product(left, right):
    return jnp.dot(left, right, preferred_element_type=jnp.float32)


def along_x(wide_ref, band):
    high, low = halves(wide_ref[...])
    for j in range(wide_ref.shape[1] // LANES - 1):
        window = slice(j * LANES, (j + 2) * LANES)
        both = product(high[:, window], band)
        yield j, both[:, :LANES] + (both[:, LANES:] + product(low[:, window], band[:, :LANES]))


def put_ahead(wide_ref, band_ref, out_refs, ny):
    per_chunk = out_refs[0].shape[2] // LANES
    for j, value in along_x(wide_ref, band_ref[...]):
        chunk, inside = divmod(j, per_chunk)
        refs = out_refs[3 * chunk:3 * chunk + 3]
        lanes = slice(inside * LANES, (inside + 1) * LANES)
        for z in range(refs[0].shape[0]):
            put(refs, z, slice(None), lanes, value[z * ny:(z + 1) * ny])


def first_body(lateral_ref, estimate_ref, *refs):
    out_refs, (wide_ref, full_ref, band_ref) = refs[:-3], refs[-3:]
    nz, ny, nx = estimate_ref.shape
    count = lateral_ref.shape[2]
    fill_band(full_ref, normalized(lambda k: lateral_ref[0, 1, k], count), 1)
    split_band(full_ref, band_ref)
    clear_edges(wide_ref)
    wide_ref[:, SHIFT:SHIFT + nx] = estimate_ref[...].reshape(nz * ny, nx)
    put_ahead(wide_ref, band_ref, out_refs, ny)


def ahead_shapes(shape, margin):
    nz, ny, nx = shape
    part = nx // CHUNKS
    return [local(nz, ny, part), local(margin, ny, part), local(margin, ny, part)] * CHUNKS


def chunked(outs):
    return [tuple(outs[3 * c:3 * c + 3]) for c in range(CHUNKS)]


def first(lateral_kernel, estimate, margin):
    nz, ny, nx = estimate.shape
    shapes = ahead_shapes(estimate.shape, margin)
    outs = pl.pallas_call(
        first_body,
        out_shape=shapes,
        in_specs=[SMEM, VMEM],
        out_specs=[VMEM] * len(shapes),
        scratch_shapes=[
            local(nz * ny, nx + LANES),
            local(2 * LANES, LANES),
            pltpu.VMEM((2 * LANES, 2 * LANES), jnp.bfloat16),
        ],
        compiler_params=LIMIT,
        name="first",
    )(lateral_kernel, pltpu.with_memory_space_constraint(estimate, pltpu.VMEM))
    return chunked(outs)


def update_body(last, taps_ref, band_ref, estimate_ref, *refs):
    halo_refs, refs = refs[:3 * CHUNKS], refs[3 * CHUNKS:]
    refs, (wide_ref, mixed_ref) = refs[:-2], refs[-2:]
    if last:
        (out_ref,) = refs
    else:
        next_ref, out_ref, *ahead_refs = refs
    nz, ny, nx = estimate_ref.shape
    per_chunk = nx // CHUNKS // LANES
    for c in range(CHUNKS):
        def store(y, j, sums):
            for z, value in enumerate(sums):
                mixed_ref[z * ny + y:z * ny + y + 8, lanes_at(j + c * per_chunk)] = value

        along_z(taps_ref, *halo_refs[3 * c:3 * c + 3], True, store)
    clear_edges(wide_ref)
    wide_ref[:, SHIFT:SHIFT + nx] = mixed_ref[...]
    for j, value in along_x(wide_ref, band_ref[...]):
        at = slice(j * LANES, (j + 1) * LANES)
        out_ref[:, :, at] = estimate_ref[:, :, at] * value.reshape(nz, ny, LANES)
    if not last:
        wide_ref[:, SHIFT:SHIFT + nx] = out_ref[...].reshape(nz * ny, nx)
        put_ahead(wide_ref, next_ref, ahead_refs, ny)


def update(taps, halos, band, estimate, band_next=None):
    nz, ny, nx = estimate.shape
    last = band_next is None
    operands = (taps, band, estimate) + sum(halos, ()) + (() if last else (band_next,))
    shapes = [local(nz, ny, nx)]
    if last:
        shapes = [jax.ShapeDtypeStruct((nz, ny, nx), jnp.float32)]
    else:
        shapes += ahead_shapes(estimate.shape, taps.shape[0] // 2)
    scratch = [local(nz * ny, nx + LANES), local(nz * ny, nx)]
    outs = call(functools.partial(update_body, last), operands, shapes, scratch)
    return outs[0], (None if last else chunked(outs[1:]))


def exchange(parts, axis):
    block, first_rows, last_rows = parts
    count = lax.axis_size(axis)
    forward = [(i, i + 1) for i in range(count - 1)]
    backward = [(target, source) for source, target in forward]
    low = lax.ppermute(last_rows, axis, forward)
    high = lax.ppermute(first_rows, axis, backward)
    return low, block, high


def pack_body(view_ref, out_ref):
    nz, nx, ny = view_ref.shape
    group = LANES // nz
    slot = lax.broadcasted_iota(jnp.int32, (8, LANES), 1) // group

    def tile(step, carry):
        t, at = step // (nx // 8), pl.ds(pl.multiple_of(step % (nx // 8) * 8, 8), 8)
        parts = [view_ref[z, at, lanes_at(t)] for z in range(nz)]
        span = nz // 2
        while span:
            odd = (slot & span) != 0
            for z in range(nz):
                if not z & span:
                    one, two = parts[z], parts[z + span]
                    parts[z] = jnp.where(odd, pltpu.roll(two, group * span, 1), one)
                    parts[z + span] = jnp.where(odd, two, pltpu.roll(one, LANES - group * span, 1))
            span //= 2
        for z in range(nz):
            out_ref[t * nz + z, at, :] = parts[z]
        return carry

    lax.fori_loop(0, ny // LANES * (nx // 8), tile, 0, unroll=True)


def unpack_body(arrived_ref, *out_refs):
    count, nx = arrived_ref.shape[0], arrived_ref.shape[1]
    nz, ny = out_refs[0].shape[1], out_refs[0].shape[0]
    flat = arrived_ref[...].reshape(count * nx, LANES)
    for j in range(count * nx // LANES):
        lanes = slice(j * LANES, (j + 1) * LANES)
        turned = jnp.swapaxes(flat[lanes].T.reshape(nz, ny, LANES), 0, 1)
        for y in range(ny):
            put(out_refs, y, slice(None), lanes, turned[y])


def halo(taps, parts, axis, reverse):
    low, block, high = exchange(parts, axis)
    return low, own(taps, block, low.shape[0], reverse), high


def reframe(view, margin):
    nz, nx, ny = view.shape
    count = lax.axis_size("row")
    rows = ny // count
    (pieces,) = call(pack_body, (view,), [local(count, nx, rows * nz)])
    arrived = lax.all_to_all(pieces, "row", 0, 0, tiled=True)
    shapes = [local(rows, nz, count * nx), local(margin, nz, count * nx), local(margin, nz, count * nx)]
    return call(unpack_body, (arrived,), shapes)


def per_device(view_a, view_b, estimate, axial_kernel, lateral_kernel):
    margin_a, margin = axial_kernel.shape[1] // 2, lateral_kernel.shape[2] // 2
    seen_a = jnp.swapaxes(view_a, 0, 1)
    seen_b = exchange(reframe(view_b, margin), "row")
    ytaps, ztaps, bands = prepare(axial_kernel, lateral_kernel)
    (ahead,) = first(lateral_kernel, estimate, margin)
    steps = 2 * ITERS
    for step in range(steps):
        v = step % 2
        yt, zt = ytaps[v], ztaps[v]
        ahead = depth(zt, *halo(zt, ahead, "col", False), False, 2 * margin if v else margin_a)
        if v:
            ahead = deep(yt, halo(yt, ahead, "row", False), seen_b, margin)
        else:
            ahead = plane(yt, *halo(yt, ahead, "row", False), False, margin_a, seen_a)
            ahead = plane(yt, *halo(yt, ahead, "row", True), True, margin)
        outer = halo(zt, ahead, "col", True)
        if step == steps - 1:
            estimate, _ = update(zt, [outer], bands[v][1], estimate)
        else:
            estimate, (ahead,) = update(zt, [outer], bands[v][1], estimate, bands[1 - v][0])
    return estimate


def solution(mesh):
    in_specs = (P("col", "row", None), P("col", "row", None), P("col", "row", None), P(), P())
    out_specs = P("col", "row", None)
    return jax.shard_map(per_device, mesh=mesh, in_specs=in_specs, out_specs=out_specs, check_vma=False)
```
